512 devices in a mesh: space: 16 (over y, z_hi), mom: 32 (over z_lo, x, core).
Axes of the slice: x: 4, y: 8, z: 8 (z_hi: 2, z_lo: 4; z = z_hi * 4 + z_lo), core: 2. Of those that a mesh axis runs over, the one named last changes fastest.
Arguments:
- density: float32 [256, 256, 2048], P('mom', None, 'space'), may hold values from -6 to 6
- mode_waves: int32 [16, 2], replicated, may hold values from -7 to 7
- mode_amplitudes: float32 [16], replicated, may hold values from -3 to 3
- mode_phases: float32 [16], replicated, may hold values from -3.140625 to 3.140625
Outputs:
- time_rate: float32 [256, 256, 2048], P('mom', None, 'space')
The draws below stay inside these ranges and needn't reach their ends.
All inputs are finite; a program needn't handle non-finite values.
Results may differ from the reference program's by a relative error of at most 0.0003.
Values sent between devices are 32-bit elements; how exact they have to be, the bound alone decides.
No kernel may reach another device: no remote copies, remote signals or barrier semaphores. Data moves between devices by JAX's collectives and lax.ppermute only.
A program may use at most 64 MiB of HBM per device.

```python
import math
import jax
import jax.numpy as jnp
from jax import lax

P_SIZE = 256
NY = 16
RX = 8
MODES = 16
NX = 128
CELLS = 2048
N_SPACE = 16


def set_ends(result, rng, least, top_value):
    dims = result.shape
    spot = [jax.random.randint(jax.random.fold_in(rng, axis), (), 0, dims[axis]) for axis in range(len(dims))]
    result = result.at[tuple(spot)].set(least)
    longest = dims.index(max(dims))
    spot[longest] = (spot[longest] + 1) % dims[longest]
    return result.at[tuple(spot)].set(top_value)


def shard_levels(rng, dims, shards, least, top_value):
    loudness = 1.0
    for axis_at, blocks in shards:
        draws = jax.random.uniform(jax.random.fold_in(jax.random.fold_in(rng, 6), axis_at), (blocks,), jnp.float32, least / len(shards), top_value / len(shards))
        loudness = loudness * jnp.repeat(jnp.exp(draws), dims[axis_at] // blocks).reshape((-1,) + (1,) * (len(dims) - 1 - axis_at))
    return loudness


def bell_draw(stream_key, dims, scale, bound, shards=(), kind=jnp.bfloat16):
    loudness = shard_levels(stream_key, dims, shards, -0.22, 0.18) if shards else 1.0
    drawn = jax.random.normal(stream_key, dims, jnp.float32) * scale * loudness
    return jnp.minimum(jnp.maximum(drawn, -bound), bound).astype(kind)


def setup_inputs(seed: int = 0) -> dict:
    key_of = jax.random.split(jax.random.key(seed), 5)
    density = bell_draw(key_of[0], (P_SIZE, P_SIZE, CELLS), 1.0, 6.0, ((0, 32), (2, 16)), jnp.float32)
    mode_waves = set_ends(jax.random.randint(key_of[1], (MODES, 2), -7, 8), jax.random.fold_in(key_of[1], 1), -7, 7).astype(jnp.int32)
    mode_amplitudes = bell_draw(key_of[2], (MODES,), 0.5, 3.0, (), jnp.float32)
    mode_phases = jnp.clip(jax.random.uniform(key_of[3], (MODES,), jnp.float32, -3.140625, 3.140625), -3.140625, 3.140625)
    return {"density": density, "mode_waves": mode_waves, "mode_amplitudes": mode_amplitudes, "mode_phases": mode_phases}


HIGHEST_PRECISION = lax.Precision.HIGHEST
DAMPING = 0.5
FRICTION = 0.5


def velocity(indices, points):
    return (2 * indices - points + 1).astype(jnp.float32) / points


def signed_frequency(indices, points):
    return jnp.where(indices < points // 2, indices, indices - points)


def cell_factors(mode_waves, mode_amplitudes, mode_phases, row_number, column_number, total_rows, total_columns):
    turn_rows = (mode_waves[:, 0:1] * row_number[None, :]) % total_rows
    turn_columns = (mode_waves[:, 1:2] * column_number[None, :]) % total_columns
    angles = 2.0 * math.pi * (turn_rows.astype(jnp.float32) / total_rows + turn_columns.astype(jnp.float32) / total_columns) + mode_phases[:, None]
    return mode_amplitudes[:, None] * jnp.sin(angles)


def freq_factors(mode_waves, first_freq, second_freq, points):
    summed = (mode_waves[None, None, :, 0] * first_freq[:, None, None] + mode_waves[None, None, :, 1] * second_freq[None, :, None]) % (2 * points)
    values = jnp.sin((math.pi / points) * summed.astype(jnp.float32))
    return values.reshape(first_freq.shape[0] * second_freq.shape[0], mode_waves.shape[0])


def damping_table(first_freq, second_freq, points):
    squares = first_freq[:, None] * first_freq[:, None] + second_freq[None, :] * second_freq[None, :]
    return (DAMPING / ((points // 2) * (points // 2))) * squares.astype(jnp.float32)


def upwind(shifted):
    minus_side = (-2.0 * shifted(-3) + 15.0 * shifted(-2) - 60.0 * shifted(-1) + 20.0 * shifted(0) + 30.0 * shifted(1) - 3.0 * shifted(2)) / 60.0
    plus_side = (2.0 * shifted(3) - 15.0 * shifted(2) + 60.0 * shifted(1) - 20.0 * shifted(0) - 30.0 * shifted(-1) + 3.0 * shifted(-2)) / 60.0
    return minus_side, plus_side


def friction_term(values, row_speeds, column_speeds):
    weighted_rows = row_speeds[:, None, None] * values
    weighted_columns = column_speeds[None, :, None] * values
    padded_rows = jnp.pad(weighted_rows, ((1, 1), (0, 0), (0, 0)))
    padded_columns = jnp.pad(weighted_columns, ((0, 0), (1, 1), (0, 0)))
    return FRICTION * ((padded_rows[2:] - padded_rows[:-2]) + (padded_columns[:, 2:] - padded_columns[:, :-2]))


def reference(density, mode_waves, mode_amplitudes, mode_phases):
    points = P_SIZE
    band_cells = RX * NY
    indices = jnp.arange(points, dtype=jnp.int32)
    signed = signed_frequency(indices, points)
    freq_factor = freq_factors(mode_waves, signed, signed, points)
    damping = damping_table(signed, signed, points)
    speeds = velocity(indices, points)

    def band_part(band_index):
        offset = (band_index * band_cells).astype(jnp.int32)
        sliced = lax.dynamic_slice_in_dim(density, offset, band_cells, 2)
        cell_ids = offset + jnp.arange(band_cells, dtype=jnp.int32)
        cell_factor = cell_factors(mode_waves, mode_amplitudes, mode_phases, cell_ids // NY, cell_ids % NY, NX, NY)
        symbol = jnp.dot(freq_factor, cell_factor, precision=HIGHEST_PRECISION).reshape(points, points, band_cells)
        spectrum = jnp.fft.fft2(sliced, axes=(0, 1))
        spectral = jnp.real(jnp.fft.ifft2((1j * symbol - damping[:, :, None]) * spectrum, axes=(0, 1)))
        return spectral + friction_term(sliced, speeds, speeds)

    momentum_part = lax.map(band_part, jnp.arange(N_SPACE, dtype=jnp.int32))

    def plane_rate(plane):
        values = lax.dynamic_index_in_dim(density, plane, 0, keepdims=False)
        moment_plane = lax.dynamic_index_in_dim(momentum_part, plane, 1, keepdims=False)
        moment_plane = jnp.moveaxis(moment_plane, 0, 1).reshape(points, CELLS)

        def across(offset):
            return jnp.roll(values, -offset * NY, axis=1)

        cell_grid = values.reshape(points, NX, NY)

        def along_row(offset):
            return jnp.roll(cell_grid, -offset, axis=2).reshape(points, CELLS)

        minus_rows, plus_rows = upwind(across)
        minus_columns, plus_columns = upwind(along_row)
        speed_rows = lax.dynamic_index_in_dim(speeds, plane, 0, keepdims=True)[:, None]
        speed_columns = speeds[:, None]
        advection = speed_rows * jnp.where(speed_rows > 0, minus_rows, plus_rows) + speed_columns * jnp.where(speed_columns > 0, minus_columns, plus_columns)
        return moment_plane - advection

    return lax.map(plane_rate, indices)
```

```python
import math

import jax
import jax.numpy as jnp
import ml_dtypes
import numpy as np
from jax import lax
from jax.experimental import pallas as pl
from jax.experimental.pallas import tpu as pltpu
from jax.sharding import PartitionSpec as P

NY = 16
POINTS = 256
HALF = POINTS // 2
DAMPING = 0.5
FRICTION = 0.5
MINUS = ((-3, -2.0), (-2, 15.0), (-1, -60.0), (0, 20.0), (1, 30.0), (2, -3.0))
PLUS = ((3, 2.0), (2, -15.0), (1, 60.0), (0, -20.0), (-1, -30.0), (-2, 3.0))
F32 = jnp.float32
BF16 = jnp.bfloat16
HIGHEST_PRECISION = lax.Precision.HIGHEST


def wide(table):
    high = table.astype(ml_dtypes.bfloat16)
    low = (table - high.astype(np.float64)).astype(ml_dtypes.bfloat16)
    return np.concatenate([high, high, low], axis=1)


def real_fourier():
    k = np.arange(POINTS)
    m = np.arange(HALF)
    angles = 2.0 * np.pi / POINTS * (m[:, None] * k[None, :] % POINTS)
    cosine, sine = np.cos(angles), -np.sin(angles)
    sine[0] = 1.0 - 2.0 * (k % 2)
    forward = np.concatenate([cosine, sine], axis=0)
    weight = np.full((HALF,), 2.0)
    weight[0] = 1.0
    inverse = (forward * np.concatenate([weight, weight])[:, None] / POINTS).T
    return forward, inverse


def interleaved(rows):
    return np.stack([rows[:HALF], rows[HALF:]], axis=1).reshape(POINTS, -1)


def friction_matrix():
    speed = (2.0 * np.arange(POINTS) - POINTS + 1) / POINTS
    result = np.zeros((POINTS, POINTS))
    k = np.arange(POINTS - 1)
    result[k, k + 1] = FRICTION * speed[k + 1]
    result[k + 1, k] = -FRICTION * speed[k]
    return result


def row_matrix(stencil, first_row, rows, out_rows):
    result = np.zeros((rows * NY, out_rows * NY))
    for out_row in range(out_rows):
        for offset, weight in stencil:
            row = out_row + offset - first_row
            if 0 <= row < rows:
                for column in range(NY):
                    result[row * NY + column, out_row * NY + column] = weight
    return result


def column_matrix(stencil, rows):
    result = np.zeros((rows * NY, rows * NY))
    for row in range(rows):
        for column in range(NY):
            for offset, weight in stencil:
                result[row * NY + (column + offset) % NY, row * NY + column] += weight
    return result


def bf16_table(table):
    return jnp.asarray(table.astype(ml_dtypes.bfloat16))


def tables(rows_dev):
    forward, inverse = real_fourier()
    result = {}
    result["forward_second"] = jnp.asarray(wide(interleaved(forward)))
    result["inverse_second"] = jnp.asarray(wide(interleaved(inverse.T).T))
    result["forward_first"] = jnp.asarray(wide(forward))
    friction = friction_matrix().astype(ml_dtypes.bfloat16)
    result["inverse_first"] = jnp.asarray(
        np.concatenate([wide(inverse), friction, friction], axis=1)
    )
    result["friction"] = jnp.asarray(np.concatenate([friction, friction], axis=1))
    rows = 2 * rows_dev
    edge = rows_dev // 2
    inner, halo = [], []
    for stencil in (PLUS, MINUS):
        inner.append(row_matrix(stencil, 0, rows, rows))
        before = row_matrix(stencil, -edge, edge, rows)
        after = row_matrix(stencil, rows, edge, rows)
        none = np.zeros_like(before)
        even = np.concatenate([before, none, after, none], axis=0)
        odd = np.concatenate([none, before, none, after], axis=0)
        halo.append(np.stack([even, odd]))
    result["row_inner"] = bf16_table(np.stack(inner))
    result["row_halo"] = bf16_table(np.stack(halo))
    result["column_shift"] = bf16_table(
        np.stack(
            [
                np.concatenate([column_matrix(s, rows_dev)] * 2, axis=0)
                for s in (PLUS, MINUS)
            ]
        )
    )
    return result


def split(value):
    high = value.astype(BF16)
    low = (value - high.astype(F32)).astype(BF16)
    return high, low


def dot(left, right):
    return jnp.dot(left, right, preferred_element_type=F32)


def speed_over_60(first, count, width):
    index = first + lax.broadcasted_iota(jnp.int32, (count, width), 0)
    return (2 * index - (POINTS - 1)).astype(F32) * (1.0 / (60 * POINTS))


def forward_kernel(u_ref, table_ref, out_ref, x_ref):
    planes, _, cells = u_ref.shape
    for k in range(planes):
        high, low = split(u_ref[k])
        x_ref[0:POINTS, k * cells : (k + 1) * cells] = high
        x_ref[POINTS : 2 * POINTS, k * cells : (k + 1) * cells] = low
    result = dot(table_ref[:, : 2 * POINTS], x_ref[...]) + dot(
        table_ref[:, 2 * POINTS :], x_ref[0:POINTS, :]
    )
    for k in range(planes):
        out_ref[pl.ds(k, POINTS, stride=planes), :] = result[:, k * cells : (k + 1) * cells]


def backward_kernel(w_ref, local_ref, table_ref, out_ref, x_ref):
    planes, _, cells = local_ref.shape
    for k in range(planes):
        high, low = split(w_ref[pl.ds(k, POINTS, stride=planes), :])
        x_ref[0:POINTS, k * cells : (k + 1) * cells] = high
        x_ref[POINTS : 2 * POINTS, k * cells : (k + 1) * cells] = low
    result = dot(table_ref[:, : 2 * POINTS], x_ref[...]) + dot(
        table_ref[:, 2 * POINTS :], x_ref[0:POINTS, :]
    )
    for k in range(planes):
        out_ref[k] = result[:, k * cells : (k + 1) * cells] + local_ref[k]


def local_kernel(u_ref, friction_ref, shift_ref, out_ref):
    planes, _, cells = u_ref.shape
    for k in range(planes):
        high, low = split(u_ref[k])
        friction = dot(friction_ref[...], jnp.concatenate([high, low], axis=0))
        both = jnp.concatenate([high, low], axis=1)
        for side in range(2):
            part = slice(side * HALF, (side + 1) * HALF)
            moved = dot(both[part], shift_ref[side])
            out_ref[k, part, :] = friction[part] - moved * speed_over_60(
                side * HALF, HALF, cells
            )


def halo_kernel(r_ref, up_ref, down_ref):
    owners = r_ref.shape[0] // 2
    cells = r_ref.shape[3]
    lower = lax.broadcasted_iota(jnp.int32, (POINTS, cells), 1) < cells // 2
    for pair in range(2):
        first, second = (
            r_ref[owners:, 2 * pair + part].reshape(POINTS, cells) for part in range(2)
        )
        up_ref[pair] = jnp.where(lower, pltpu.roll(first, cells // 2, 1), second)
        first, second = (
            r_ref[:owners, 2 * pair + part].reshape(POINTS, cells) for part in range(2)
        )
        down_ref[pair] = jnp.where(lower, first, pltpu.roll(second, cells // 2, 1))


def load_columns(r_ref, x_ref):
    owners = r_ref.shape[0] // 2
    cells = r_ref.shape[3]
    for q in range(4):
        for side in range(2):
            value = r_ref[side * owners : (side + 1) * owners, q].reshape(POINTS, cells)
            high, low = split(value)
            at = (2 * q + side) * cells
            x_ref[0:POINTS, at : at + cells] = high
            x_ref[POINTS : 2 * POINTS, at : at + cells] = low


def spectral_kernel(damp_ref, r_ref, table_ref, symbol_ref, x_ref, y_ref):
    load_columns(r_ref, x_ref)
    spectrum = dot(table_ref[:, : 2 * POINTS], x_ref[...]) + dot(
        table_ref[:, 2 * POINTS :], x_ref[0:POINTS, :]
    )
    width = spectrum.shape[1] // 4
    row = lax.broadcasted_iota(jnp.int32, (HALF, width), 0)
    scale = DAMPING / (HALF * HALF)
    damp_real = scale * (row * row).astype(F32)
    row_imag = jnp.where(row == 0, HALF, row)
    damp_imag = scale * (row_imag * row_imag).astype(F32)
    for slot in range(2):
        qa, qb = 2 * slot, 2 * slot + 1
        real_a, imag_a = (
            spectrum[h * HALF : (h + 1) * HALF, qa * width : (qa + 1) * width]
            for h in range(2)
        )
        real_b, imag_b = (
            spectrum[h * HALF : (h + 1) * HALF, qb * width : (qb + 1) * width]
            for h in range(2)
        )
        odd_a, odd_b = symbol_ref[slot, 0], symbol_ref[slot, 1]
        even_real, even_imag = symbol_ref[slot, 2], symbol_ref[slot, 3]
        da, db = damp_ref[qa], damp_ref[qb]
        results = (
            (qa, 0, -odd_a * imag_a - even_real * real_b - (damp_real + da) * real_a),
            (qa, 1, odd_a * real_a - even_imag * imag_b - (damp_imag + da) * imag_a),
            (qb, 0, -odd_b * imag_b + even_real * real_a - (damp_real + db) * real_b),
            (qb, 1, odd_b * real_b + even_imag * imag_a - (damp_imag + db) * imag_b),
        )
        for q, half, value in results:
            high, low = split(value)
            at = q * width
            y_ref[half * HALF : (half + 1) * HALF, at : at + width] = high
            y_ref[POINTS + half * HALF : POINTS + (half + 1) * HALF, at : at + width] = low


def combine_kernel(x_ref, y_ref, before_ref, after_ref, table_ref, inner_ref, halo_ref, out_ref):
    width = x_ref.shape[1] // 4
    cells = width // 2
    owners = out_ref.shape[0] // 2
    result = (
        dot(table_ref[:, : 2 * POINTS], y_ref[...])
        + dot(table_ref[:, 2 * POINTS : 3 * POINTS], y_ref[0:POINTS, :])
        + dot(table_ref[:, 3 * POINTS :], x_ref[...])
    )
    halos = []
    for pair in range(2):
        before_high, before_low = split(before_ref[pair])
        after_high, after_low = split(after_ref[pair])
        halos.append(
            (
                jnp.concatenate([before_high, after_high], axis=1),
                jnp.concatenate([before_low, after_low], axis=1),
            )
        )
    for q in range(4):
        columns = slice(q * width, (q + 1) * width)
        for side in range(2):
            part = slice(side * HALF, (side + 1) * HALF)
            low = slice(POINTS + side * HALF, POINTS + (side + 1) * HALF)
            inner, halo = inner_ref[side], halo_ref[side, q % 2]
            high_halo, low_halo = halos[q // 2]
            moved = (
                dot(x_ref[part, columns], inner)
                + dot(x_ref[low, columns], inner)
                + dot(high_halo[part], halo)
                + dot(low_halo[part], halo)
            )
            value = result[part, columns] - moved * speed_over_60(side * HALF, HALF, width)
            rows = owners // 2
            for band in range(2):
                out_ref[
                    band * owners + side * rows : band * owners + (side + 1) * rows, q
                ] = value[:, band * cells : (band + 1) * cells].reshape(rows, -1, cells)


VMEM_SPEC = pl.BlockSpec(memory_space=pltpu.VMEM)
SMEM_SPEC = pl.BlockSpec(memory_space=pltpu.SMEM)


def call(kernel, shapes, inputs, scratch=(), flops=1, smem=0, name=None):
    bytes_accessed = sum(v.size * v.dtype.itemsize for v in inputs)
    shapes = [jax.ShapeDtypeStruct(*s) for s in shapes]
    single = len(shapes) == 1
    return pl.pallas_call(
        kernel,
        out_shape=shapes[0] if single else shapes,
        in_specs=[SMEM_SPEC] * smem + [VMEM_SPEC] * (len(inputs) - smem),
        out_specs=VMEM_SPEC if single else [VMEM_SPEC] * len(shapes),
        scratch_shapes=list(scratch),
        cost_estimate=pl.CostEstimate(
            flops=flops, bytes_accessed=2 * bytes_accessed, transcendentals=0
        ),
        name=name,
    )(*inputs)


def symbol_table(mode_waves, mode_amplitudes, mode_phases, first_slot, first_row, rows, total_rows):
    local = jnp.arange(rows * NY, dtype=jnp.int32)
    row, column = first_row + local // NY, local % NY
    turn_rows = mode_waves[:, 0:1] * row[None, :] % total_rows
    turn_columns = mode_waves[:, 1:2] * column[None, :] % NY
    angles = (
        2.0
        * math.pi
        * (turn_rows.astype(F32) / total_rows + turn_columns.astype(F32) / NY)
        + mode_phases[:, None]
    )
    cell_factor = mode_amplitudes[:, None] * jnp.sin(angles)
    scale = math.pi / POINTS

    def turned(waves, frequency):
        return scale * (waves * frequency % (2 * POINTS)).astype(F32)

    first_waves, second_waves = mode_waves[None, :, 0], mode_waves[None, :, 1]
    real_freq = jnp.arange(HALF, dtype=jnp.int32)[:, None]
    imag_freq = jnp.where(real_freq == 0, HALF, real_freq)
    odd_first = jnp.sin(turned(first_waves, real_freq))
    even_real = jnp.cos(turned(first_waves, real_freq))
    even_imag = jnp.cos(turned(first_waves, imag_freq))
    slots = first_slot + jnp.arange(2, dtype=jnp.int32)[:, None]
    slots_b = jnp.where(slots == 0, HALF, slots)
    odd_second = jnp.sin(turned(second_waves, slots))
    even_a = jnp.cos(turned(second_waves, slots))
    even_b = jnp.cos(turned(second_waves, slots_b))
    factors = jnp.stack(
        [
            odd_first[None] * even_a[:, None],
            odd_first[None] * even_b[:, None],
            even_real[None] * odd_second[:, None],
            even_imag[None] * odd_second[:, None],
        ],
        axis=1,
    )
    symbol = jnp.dot(
        factors.reshape(8 * HALF, -1), cell_factor, precision=HIGHEST_PRECISION
    ).reshape(2, 4, HALF, rows * NY)
    damp = DAMPING / (HALF * HALF) * jnp.stack(
        [slots * slots, slots_b * slots_b], axis=1
    ).reshape(4).astype(F32)
    return symbol, damp


def stage_forward(density, table):
    planes, points, cells = density.shape
    width = planes * cells
    sent = call(
        forward_kernel,
        [((points * planes, cells), F32)],
        (density, table["forward_second"]),
        (pltpu.VMEM((2 * points, width), BF16),),
        6 * points * points * width,
        name="forward_second",
    )
    return sent.reshape(points // 4, 4, planes, cells)


def stage_local(density, table):
    planes, points, cells = density.shape
    return call(
        local_kernel,
        [((planes, points, cells), F32)],
        (density, table["friction"], table["column_shift"]),
        flops=6 * points * points * planes * cells,
        name="local_part",
    )


def stage_halo(columns):
    cells = columns.shape[3]
    return call(
        halo_kernel, [((2, POINTS, cells), F32)] * 2, (columns,), name="halo_pack"
    )


def stage_spectral(damp, columns, symbol, table):
    width = 8 * columns.shape[3]
    return call(
        spectral_kernel,
        [((2 * POINTS, width), BF16)] * 2,
        (damp, columns, table["forward_first"], symbol),
        flops=6 * POINTS * POINTS * width,
        smem=1,
        name="spectral",
    )


def stage_combine(x, y, before, after, table, planes, members):
    width = x.shape[1]
    return call(
        combine_kernel,
        [((members, 4, planes, width // 8), F32)],
        (x, y, before, after, table["inverse_first"], table["row_inner"], table["row_halo"]),
        flops=18 * POINTS * POINTS * width,
        name="combine",
    )


def stage_backward(panels, here, table):
    planes, points, cells = here.shape
    width = planes * cells
    return call(
        backward_kernel,
        [((planes, points, cells), F32)],
        (panels.reshape(points * planes, cells), here, table["inverse_second"]),
        (pltpu.VMEM((2 * points, width), BF16),),
        6 * points * points * width,
        name="inverse_second",
    )


def local(density, mode_waves, mode_amplitudes, mode_phases):
    planes, _, cells = density.shape
    rows_dev = cells // NY
    group = ("pair", "mom")
    members = lax.axis_size(group)
    strips = lax.axis_size("y")
    table = tables(rows_dev)

    sent = stage_forward(density, table)
    columns = lax.all_to_all(sent, group, split_axis=0, concat_axis=0, tiled=True)
    here = stage_local(density, table)
    position = lax.axis_index("pair") * lax.axis_size("mom") + lax.axis_index("mom")
    symbol, damp = symbol_table(
        mode_waves,
        mode_amplitudes,
        mode_phases,
        2 * position,
        lax.axis_index("y") * (2 * rows_dev),
        2 * rows_dev,
        2 * rows_dev * strips,
    )
    up, down = stage_halo(columns)
    before = lax.ppermute(up, "y", [(i, (i + 1) % strips) for i in range(strips)])
    after = lax.ppermute(down, "y", [((i + 1) % strips, i) for i in range(strips)])
    x, y = stage_spectral(damp, columns, symbol, table)
    back = stage_combine(x, y, before, after, table, planes, members)
    panels = lax.all_to_all(back, group, split_axis=0, concat_axis=0, tiled=True)
    return stage_backward(panels, here, table)


def solution(mesh):
    bands = mesh.shape["space"]
    finer = jax.sharding.Mesh(
        mesh.devices.reshape(bands // 2, 2, mesh.shape["mom"]), ("y", "pair", "mom")
    )
    return jax.shard_map(
        local,
        mesh=finer,
        in_specs=(P("mom", None, ("y", "pair")), P(), P(), P()),
        out_specs=P("mom", None, ("y", "pair")),
        check_vma=False,
    )
```

```python
import math

import jax
import jax.numpy as jnp
import ml_dtypes
import numpy as np
from jax import lax
from jax.experimental import pallas as pl
from jax.experimental.pallas import tpu as pltpu
from jax.sharding import PartitionSpec as P

NY = 16
POINTS = 256
HALF = POINTS // 2
DAMPING = 0.5
FRICTION = 0.5
MINUS = ((-3, -2.0), (-2, 15.0), (-1, -60.0), (0, 20.0), (1, 30.0), (2, -3.0))
PLUS = ((3, 2.0), (2, -15.0), (1, 60.0), (0, -20.0), (-1, -30.0), (-2, 3.0))
F32 = jnp.float32
BF16 = jnp.bfloat16
HIGHEST_PRECISION = lax.Precision.HIGHEST
FORWARD_STEPS = 4
BACKWARD_STEPS = 2
SENT_ON_CHIP = True


def wide(table):
    high = table.astype(ml_dtypes.bfloat16)
    low = (table - high.astype(np.float64)).astype(ml_dtypes.bfloat16)
    return np.concatenate([high, high, low], axis=1)


def real_fourier():
    k = np.arange(POINTS)
    m = np.arange(HALF)
    angles = 2.0 * np.pi / POINTS * (m[:, None] * k[None, :] % POINTS)
    cosine, sine = np.cos(angles), -np.sin(angles)
    sine[0] = 1.0 - 2.0 * (k % 2)
    forward = np.concatenate([cosine, sine], axis=0)
    weight = np.full((HALF,), 2.0)
    weight[0] = 1.0
    inverse = (forward * np.concatenate([weight, weight])[:, None] / POINTS).T
    return forward, inverse


def interleaved(rows):
    return np.stack([rows[:HALF], rows[HALF:]], axis=1).reshape(POINTS, -1)


def friction_matrix():
    speed = (2.0 * np.arange(POINTS) - POINTS + 1) / POINTS
    result = np.zeros((POINTS, POINTS))
    k = np.arange(POINTS - 1)
    result[k, k + 1] = FRICTION * speed[k + 1]
    result[k + 1, k] = -FRICTION * speed[k]
    return result


def row_matrix(stencil, rows):
    result = np.zeros((rows * NY, rows * NY))
    for out_row in range(rows):
        for offset, weight in stencil:
            row = out_row + offset
            if 0 <= row < rows:
                for column in range(NY):
                    result[row * NY + column, out_row * NY + column] = weight
    return result


def column_matrix(stencil, rows):
    result = np.zeros((rows * NY, rows * NY))
    for row in range(rows):
        for column in range(NY):
            for offset, weight in stencil:
                result[row * NY + (column + offset) % NY, row * NY + column] += weight
    return result


def bf16_table(table):
    return jnp.asarray(table.astype(ml_dtypes.bfloat16))


def tables(rows_dev):
    forward, inverse = real_fourier()
    result = {}
    result["forward_second"] = jnp.asarray(wide(interleaved(forward)))
    result["inverse_second"] = jnp.asarray(wide(interleaved(inverse.T).T))
    result["forward_first"] = jnp.asarray(wide(forward))
    friction = friction_matrix().astype(ml_dtypes.bfloat16)
    result["inverse_first"] = jnp.asarray(
        np.concatenate([wide(inverse), friction, friction], axis=1)
    )
    result["friction"] = jnp.asarray(np.concatenate([friction, friction], axis=1))
    rows = 2 * rows_dev
    result["row_inner"] = bf16_table(
        np.stack([row_matrix(stencil, rows) for stencil in (PLUS, MINUS)])
    )
    result["column_shift"] = bf16_table(
        np.stack(
            [
                np.concatenate([column_matrix(s, rows_dev)] * 2, axis=0)
                for s in (PLUS, MINUS)
            ]
        )
    )
    return result


def split(value):
    high = value.astype(BF16)
    low = (value - high.astype(F32)).astype(BF16)
    return high, low


def dot(left, right):
    return jnp.dot(left, right, preferred_element_type=F32)


def speed_over_60(first, count, width):
    index = first + lax.broadcasted_iota(jnp.int32, (count, width), 0)
    return (2 * index - (POINTS - 1)).astype(F32) * (1.0 / (60 * POINTS))


def forward_kernel(u_ref, table_ref, out_ref):
    planes, _, cells = u_ref.shape
    first = pl.program_id(0) * planes
    parts = [split(u_ref[k]) for k in range(planes)]
    high, low = (jnp.concatenate(values, axis=1) for values in zip(*parts))
    result = dot(table_ref[:, : 2 * POINTS], jnp.concatenate([high, low], axis=0)) + dot(
        table_ref[:, 2 * POINTS :], high
    )
    stride = out_ref.shape[0] // POINTS
    for k in range(planes):
        out_ref[pl.ds(first + k, POINTS, stride=stride), :] = result[
            :, k * cells : (k + 1) * cells
        ]


def backward_kernel(w_ref, local_ref, table_ref, out_ref):
    planes, _, cells = out_ref.shape
    first = pl.program_id(0) * planes
    stride = w_ref.shape[0] // POINTS
    parts = [
        split(w_ref[pl.ds(first + k, POINTS, stride=stride), :]) for k in range(planes)
    ]
    high, low = (jnp.concatenate(values, axis=1) for values in zip(*parts))
    result = dot(table_ref[:, : 2 * POINTS], jnp.concatenate([high, low], axis=0)) + dot(
        table_ref[:, 2 * POINTS :], high
    )
    for k in range(planes):
        out_ref[k] = result[:, k * cells : (k + 1) * cells] + local_ref[first + k]


def local_kernel(u_ref, friction_ref, shift_ref, out_ref):
    planes, _, cells = u_ref.shape
    for k in range(planes):
        high, low = split(u_ref[k])
        friction = dot(friction_ref[...], jnp.concatenate([high, low], axis=0))
        both = jnp.concatenate([high, low], axis=1)
        for side in range(2):
            part = slice(side * HALF, (side + 1) * HALF)
            moved = dot(both[part], shift_ref[side])
            out_ref[k, part, :] = friction[part] - moved * speed_over_60(
                side * HALF, HALF, cells
            )


def lane_select(values, lane, width):
    result = values[0]
    for index, value in enumerate(values[1:], 1):
        result = jnp.where(lane >= index * width, value, result)
    return result


def turn(value, shift):
    shift %= value.shape[1]
    return pltpu.roll(value, shift, 1) if shift else value


def pack(r_ref, near, far, side):
    cells = r_ref.shape[3]
    lane = lax.broadcasted_iota(jnp.int32, (POINTS, cells), 1)
    columns = [r_ref[:, q].reshape(POINTS, cells) for q in range(4)]
    wide_part = lane_select(
        [turn(v, 2 * NY * q - near) for q, v in enumerate(columns)], lane, 2 * NY
    )
    quarter = HALF // 2
    lane = lane[:quarter]
    thin_part = lane_select(
        [
            turn(columns[q][side * HALF + h * quarter : side * HALF + (h + 1) * quarter], NY * (q + 4 * h) - far)
            for h in range(2)
            for q in range(4)
        ],
        lane,
        NY,
    )
    return wide_part, thin_part


def halo_kernel(odd_ref, r_ref, first_ref, second_ref):
    owners = r_ref.shape[0] // 2
    cells = r_ref.shape[3]
    odd = odd_ref[0] == 1
    up = pack(r_ref.at[owners:], cells - 2 * NY, cells - 3 * NY, 1)
    down = pack(r_ref.at[:owners], 0, 2 * NY, 0)
    at = 0
    for upper, lower in zip(up, down):
        rows = upper.shape[0]
        first_ref[at : at + rows, :] = jnp.where(odd, lower, upper)
        second_ref[at : at + rows, :] = jnp.where(odd, upper, lower)
        at += rows


def load_columns(r_ref, x_ref):
    owners = r_ref.shape[0] // 2
    cells = r_ref.shape[3]
    for q in range(4):
        for side in range(2):
            value = r_ref[side * owners : (side + 1) * owners, q].reshape(POINTS, cells)
            high, low = split(value)
            at = (2 * q + side) * cells
            x_ref[0:POINTS, at : at + cells] = high
            x_ref[POINTS : 2 * POINTS, at : at + cells] = low


def middle_kernel(damp_ref, r_ref, forward_ref, symbol_ref, inverse_ref, inner_ref, out_ref, x_ref, y_ref):
    load_columns(r_ref, x_ref)
    spectrum = dot(forward_ref[:, : 2 * POINTS], x_ref[...]) + dot(
        forward_ref[:, 2 * POINTS :], x_ref[0:POINTS, :]
    )
    width = spectrum.shape[1] // 4
    row = lax.broadcasted_iota(jnp.int32, (HALF, width), 0)
    scale = DAMPING / (HALF * HALF)
    damp_real = scale * (row * row).astype(F32)
    row_imag = jnp.where(row == 0, HALF, row)
    damp_imag = scale * (row_imag * row_imag).astype(F32)
    for slot in range(2):
        qa, qb = 2 * slot, 2 * slot + 1
        real_a, imag_a = (
            spectrum[h * HALF : (h + 1) * HALF, qa * width : (qa + 1) * width]
            for h in range(2)
        )
        real_b, imag_b = (
            spectrum[h * HALF : (h + 1) * HALF, qb * width : (qb + 1) * width]
            for h in range(2)
        )
        odd_a, odd_b = symbol_ref[slot, 0], symbol_ref[slot, 1]
        even_real, even_imag = symbol_ref[slot, 2], symbol_ref[slot, 3]
        da, db = damp_ref[qa], damp_ref[qb]
        results = (
            (qa, 0, -odd_a * imag_a - even_real * real_b - (damp_real + da) * real_a),
            (qa, 1, odd_a * real_a - even_imag * imag_b - (damp_imag + da) * imag_a),
            (qb, 0, -odd_b * imag_b + even_real * real_a - (damp_real + db) * real_b),
            (qb, 1, odd_b * real_b + even_imag * imag_a - (damp_imag + db) * imag_b),
        )
        for q, half, value in results:
            high, low = split(value)
            at = q * width
            y_ref[half * HALF : (half + 1) * HALF, at : at + width] = high
            y_ref[POINTS + half * HALF : POINTS + (half + 1) * HALF, at : at + width] = low
    cells = width // 2
    owners = out_ref.shape[0] // 2
    result = (
        dot(inverse_ref[:, : 2 * POINTS], y_ref[...])
        + dot(inverse_ref[:, 2 * POINTS : 3 * POINTS], y_ref[0:POINTS, :])
        + dot(inverse_ref[:, 3 * POINTS :], x_ref[...])
    )
    for side in range(2):
        part = slice(side * HALF, (side + 1) * HALF)
        low_part = slice(POINTS + side * HALF, POINTS + (side + 1) * HALF)
        moved = sum(
            dot(
                jnp.concatenate(
                    [x_ref[rows, q * width : (q + 1) * width] for q in range(4)], axis=0
                ),
                inner_ref[side],
            )
            for rows in (part, low_part)
        )
        speed = speed_over_60(side * HALF, HALF, width)
        rows = owners // 2
        for q in range(4):
            value = (
                result[part, q * width : (q + 1) * width]
                - moved[q * HALF : (q + 1) * HALF] * speed
            )
            for band in range(2):
                out_ref[
                    band * owners + side * rows : band * owners + (side + 1) * rows, q
                ] = value[:, band * cells : (band + 1) * cells].reshape(rows, -1, cells)


def lane_weight(lane, first_row, last_row, weight):
    return jnp.where((lane >= first_row * NY) & (lane < last_row * NY), weight, 0.0)


def edge_kernel(odd_ref, partial_ref, first_ref, second_ref, out_ref):
    owners = out_ref.shape[0] // 2
    cells = out_ref.shape[3]
    odd = odd_ref[0] == 1
    band_rows = cells // NY
    quarter = HALF // 2
    half_owners = owners // 2
    lane = lax.broadcasted_iota(jnp.int32, (HALF, cells), 1)

    def both(rows):
        return first_ref[rows, :], second_ref[rows, :]

    thin_first, thin_second = both(slice(POINTS, POINTS + quarter))
    for side, stencil in enumerate((PLUS, MINUS)):
        weights = dict(stencil)
        one, two = both(slice(side * HALF, (side + 1) * HALF))
        before, after = jnp.where(odd, one, two), jnp.where(odd, two, one)
        if side:
            thin = jnp.where(odd, thin_first, thin_second)
        else:
            thin = jnp.where(odd, thin_second, thin_first)
        speed = speed_over_60(side * HALF, HALF, cells)
        low = slice(side * half_owners, (side + 1) * half_owners)
        high = slice(owners + side * half_owners, owners + (side + 1) * half_owners)
        for q in range(4):
            moved_low = moved_high = 0.0
            for s in range(1, 4 if side else 3):
                moved_low += lane_weight(lane, max(s - 2, 0), s, weights[-s]) * turn(
                    before, NY * (s - 2 - 2 * q)
                )
            for s in range(1, 3 if side else 4):
                top = band_rows - s
                moved_high += lane_weight(
                    lane, top, min(top + 2, band_rows), weights[s]
                ) * turn(after, NY * (top - 2 * q))
            third = jnp.concatenate(
                [
                    turn(thin, NY * ((0 if side else band_rows - 1) - q - 4 * h))
                    for h in range(2)
                ],
                axis=0,
            )
            if side:
                moved_low += lane_weight(lane, 0, 1, weights[-3]) * third
            else:
                moved_high += lane_weight(lane, band_rows - 1, band_rows, weights[3]) * third
            out_ref[low, q] = partial_ref[low, q] - (moved_low * speed).reshape(
                half_owners, -1, cells
            )
            out_ref[high, q] = partial_ref[high, q] - (moved_high * speed).reshape(
                half_owners, -1, cells
            )


VMEM_SPEC = pl.BlockSpec(memory_space=pltpu.VMEM)
SMEM_SPEC = pl.BlockSpec(memory_space=pltpu.SMEM)


def on_chip(value):
    return pltpu.with_memory_space_constraint(value, pltpu.VMEM)


def call(
    kernel,
    shapes,
    inputs,
    scratch=(),
    flops=1,
    smem=0,
    keep=True,
    grid=(),
    in_specs=None,
    out_specs=None,
):
    bytes_accessed = sum(v.size * v.dtype.itemsize for v in inputs)
    shapes = [pltpu.VMEM(*s) if keep else jax.ShapeDtypeStruct(*s) for s in shapes]
    if in_specs is None:
        inputs = [*inputs[:smem], *(on_chip(v) for v in inputs[smem:])]
        in_specs = [SMEM_SPEC] * smem + [VMEM_SPEC] * (len(inputs) - smem)
    if out_specs is None:
        out_specs = [VMEM_SPEC] * len(shapes)
    single = len(shapes) == 1
    return pl.pallas_call(
        kernel,
        grid=grid,
        out_shape=shapes[0] if single else shapes,
        in_specs=in_specs,
        out_specs=out_specs[0] if single else out_specs,
        scratch_shapes=list(scratch),
        cost_estimate=pl.CostEstimate(
            flops=flops, bytes_accessed=2 * bytes_accessed, transcendentals=0
        ),
        compiler_params=pltpu.CompilerParams(vmem_limit_bytes=24 << 20),
    )(*inputs)


def symbol_table(mode_waves, mode_amplitudes, mode_phases, first_slot, first_row, rows, total_rows):
    local = jnp.arange(rows * NY, dtype=jnp.int32)
    row, column = first_row + local // NY, local % NY
    turn_rows = mode_waves[:, 0:1] * row[None, :] % total_rows
    turn_columns = mode_waves[:, 1:2] * column[None, :] % NY
    angles = (
        2.0
        * math.pi
        * (turn_rows.astype(F32) / total_rows + turn_columns.astype(F32) / NY)
        + mode_phases[:, None]
    )
    cell_factor = mode_amplitudes[:, None] * jnp.sin(angles)
    scale = math.pi / POINTS

    def turned(waves, frequency):
        return scale * (waves * frequency % (2 * POINTS)).astype(F32)

    first_waves, second_waves = mode_waves[None, :, 0], mode_waves[None, :, 1]
    real_freq = jnp.arange(HALF, dtype=jnp.int32)[:, None]
    imag_freq = jnp.where(real_freq == 0, HALF, real_freq)
    odd_first = jnp.sin(turned(first_waves, real_freq))
    even_real = jnp.cos(turned(first_waves, real_freq))
    even_imag = jnp.cos(turned(first_waves, imag_freq))
    slots = first_slot + jnp.arange(2, dtype=jnp.int32)[:, None]
    slots_b = jnp.where(slots == 0, HALF, slots)
    odd_second = jnp.sin(turned(second_waves, slots))
    even_a = jnp.cos(turned(second_waves, slots))
    even_b = jnp.cos(turned(second_waves, slots_b))
    factors = jnp.stack(
        [
            odd_first[None] * even_a[:, None],
            odd_first[None] * even_b[:, None],
            even_real[None] * odd_second[:, None],
            even_imag[None] * odd_second[:, None],
        ],
        axis=1,
    )
    symbol = jnp.dot(
        factors.reshape(8 * HALF, -1), cell_factor, precision=HIGHEST_PRECISION
    ).reshape(2, 4, HALF, rows * NY)
    damp = DAMPING / (HALF * HALF) * jnp.stack(
        [slots * slots, slots_b * slots_b], axis=1
    ).reshape(4).astype(F32)
    return symbol, damp


def stage_forward(density, table, keep=SENT_ON_CHIP):
    planes, points, cells = density.shape
    sent = call(
        forward_kernel,
        [((points * planes, cells), F32)],
        (density, table["forward_second"]),
        flops=6 * points * points * planes * cells,
        keep=keep,
        grid=(FORWARD_STEPS,),
        in_specs=[
            pl.BlockSpec((planes // FORWARD_STEPS, points, cells), lambda i: (i, 0, 0)),
            pl.BlockSpec((points, 3 * points), lambda i: (0, 0)),
        ],
        out_specs=[VMEM_SPEC if keep else pl.BlockSpec((points * planes, cells), lambda i: (0, 0))],
    )
    return sent.reshape(points // 4, 4, planes, cells)


def stage_local(density, table):
    planes, points, cells = density.shape
    return call(
        local_kernel,
        [((planes, points, cells), F32)],
        (density, table["friction"], table["column_shift"]),
        flops=6 * points * points * planes * cells,
    )


def stage_halo(odd, columns):
    cells = columns.shape[3]
    return call(
        halo_kernel, [((POINTS + POINTS // 4, cells), F32)] * 2, (odd, columns), smem=1
    )


def stage_middle(damp, columns, symbol, table):
    _, _, _, cells = columns.shape
    width = 8 * cells
    scratch = pltpu.VMEM((2 * POINTS, width), BF16)
    return call(
        middle_kernel,
        [(columns.shape, F32)],
        (
            damp,
            columns,
            table["forward_first"],
            symbol,
            table["inverse_first"],
            table["row_inner"],
        ),
        (scratch, scratch),
        20 * POINTS * POINTS * width,
        smem=1,
    )


def stage_edge(odd, partial, first, second, keep=SENT_ON_CHIP):
    return call(
        edge_kernel,
        [(partial.shape, F32)],
        (odd, partial, first, second),
        flops=40 * partial.size,
        smem=1,
        keep=keep,
    )


def stage_backward(panels, here, table):
    planes, points, cells = here.shape
    return call(
        backward_kernel,
        [((planes, points, cells), F32)],
        (
            on_chip(panels.reshape(points * planes, cells)),
            on_chip(here),
            on_chip(table["inverse_second"]),
        ),
        flops=6 * points * points * planes * cells,
        keep=False,
        grid=(BACKWARD_STEPS,),
        in_specs=[VMEM_SPEC] * 3,
        out_specs=[
            pl.BlockSpec((planes // BACKWARD_STEPS, points, cells), lambda i: (i, 0, 0))
        ],
    )


def local(density, mode_waves, mode_amplitudes, mode_phases):
    _, _, cells = density.shape
    rows_dev = cells // NY
    group = ("pair", "mom")
    strips = lax.axis_size("y")
    table = tables(rows_dev)

    sent = stage_forward(density, table)
    columns = lax.all_to_all(sent, group, split_axis=0, concat_axis=0, tiled=True)
    here = stage_local(density, table)
    position = lax.axis_index("pair") * lax.axis_size("mom") + lax.axis_index("mom")
    odd = (lax.axis_index("y") % 2).reshape(1)
    symbol, damp = symbol_table(
        mode_waves,
        mode_amplitudes,
        mode_phases,
        2 * position,
        lax.axis_index("y") * (2 * rows_dev),
        2 * rows_dev,
        2 * rows_dev * strips,
    )
    first, second = stage_halo(odd, columns)
    links = [(i, (i + 1) % strips) for i in range(strips)]
    swaps = [[p for l in links[start::2] for p in (l, l[::-1])] for start in range(2)]
    first = lax.ppermute(first, "y", swaps[0])
    second = lax.ppermute(second, "y", swaps[1])
    partial = stage_middle(damp, columns, symbol, table)
    back = stage_edge(odd, partial, first, second)
    panels = lax.all_to_all(back, group, split_axis=0, concat_axis=0, tiled=True)
    return stage_backward(panels, here, table)


def solution(mesh):
    bands = mesh.shape["space"]
    finer = jax.sharding.Mesh(
        mesh.devices.reshape(bands // 2, 2, mesh.shape["mom"]), ("y", "pair", "mom")
    )
    return jax.shard_map(
        local,
        mesh=finer,
        in_specs=(P("mom", None, ("y", "pair")), P(), P(), P()),
        out_specs=P("mom", None, ("y", "pair")),
        check_vma=False,
    )
```

```python
import math

import jax
import jax.numpy as jnp
import ml_dtypes
import numpy as np
from jax import lax
from jax.experimental import pallas as pl
from jax.experimental.pallas import tpu as pltpu
from jax.sharding import PartitionSpec as P

NY = 16
POINTS = 256
HALF = POINTS // 2
DAMPING = 0.5
FRICTION = 0.5
MINUS = ((-3, -2.0), (-2, 15.0), (-1, -60.0), (0, 20.0), (1, 30.0), (2, -3.0))
PLUS = ((3, 2.0), (2, -15.0), (1, 60.0), (0, -20.0), (-1, -30.0), (-2, 3.0))
F32 = jnp.float32
BF16 = jnp.bfloat16
HIGHEST_PRECISION = lax.Precision.HIGHEST
FORWARD_STEPS = 4
BACKWARD_STEPS = 2


def wide(table):
    high = table.astype(ml_dtypes.bfloat16)
    low = (table - high.astype(np.float64)).astype(ml_dtypes.bfloat16)
    return np.concatenate([high, low], axis=1)


def real_fourier():
    k = np.arange(POINTS)
    m = np.arange(HALF)
    angles = 2.0 * np.pi / POINTS * (m[:, None] * k[None, :] % POINTS)
    cosine, sine = np.cos(angles), -np.sin(angles)
    sine[0] = 1.0 - 2.0 * (k % 2)
    forward = np.concatenate([cosine, sine], axis=0)
    weight = np.full((HALF,), 2.0)
    weight[0] = 1.0
    inverse = (forward * np.concatenate([weight, weight])[:, None] / POINTS).T
    return forward, inverse


def interleaved(rows):
    return np.stack([rows[:HALF], rows[HALF:]], axis=1).reshape(POINTS, -1)


def friction_matrix():
    speed = (2.0 * np.arange(POINTS) - POINTS + 1) / POINTS
    result = np.zeros((POINTS, POINTS))
    k = np.arange(POINTS - 1)
    result[k, k + 1] = FRICTION * speed[k + 1]
    result[k + 1, k] = -FRICTION * speed[k]
    return result


def row_matrix(stencil, rows):
    result = np.zeros((rows * NY, rows * NY))
    for out_row in range(rows):
        for offset, weight in stencil:
            row = out_row + offset
            if 0 <= row < rows:
                for column in range(NY):
                    result[row * NY + column, out_row * NY + column] = weight
    return result


def column_matrix(stencil, rows):
    result = np.zeros((rows * NY, rows * NY))
    for row in range(rows):
        for column in range(NY):
            for offset, weight in stencil:
                result[row * NY + (column + offset) % NY, row * NY + column] += weight
    return result


def bf16_table(table):
    return jnp.asarray(table.astype(ml_dtypes.bfloat16))


def tables(rows_dev):
    forward, inverse = real_fourier()
    result = {}
    result["forward_second"] = jnp.asarray(wide(interleaved(forward)))
    result["inverse_second"] = jnp.asarray(wide(interleaved(inverse.T).T))
    result["forward_first"] = jnp.asarray(wide(forward))
    friction = friction_matrix().astype(ml_dtypes.bfloat16)
    result["inverse_first"] = jnp.asarray(
        np.concatenate([wide(inverse), friction], axis=1)
    )
    result["friction"] = jnp.asarray(np.concatenate([friction, friction], axis=1))
    rows = 2 * rows_dev
    result["row_inner"] = bf16_table(
        np.stack([row_matrix(stencil, rows) for stencil in (PLUS, MINUS)])
    )
    result["column_shift"] = bf16_table(
        np.stack(
            [
                np.concatenate([column_matrix(s, rows_dev)] * 2, axis=0)
                for s in (PLUS, MINUS)
            ]
        )
    )
    return result


def split(value):
    high = value.astype(BF16)
    low = (value - high.astype(F32)).astype(BF16)
    return high, low


def dot(left, right):
    return jnp.dot(left, right, preferred_element_type=F32)


def wide_dot(table, high, low):
    return (
        dot(table[:, :POINTS], high)
        + dot(table[:, :POINTS], low)
        + dot(table[:, POINTS : 2 * POINTS], high)
    )


def speed_over_60(first, count, width):
    index = first + lax.broadcasted_iota(jnp.int32, (count, width), 0)
    return (2 * index - (POINTS - 1)).astype(F32) * (1.0 / (60 * POINTS))


def forward_kernel(u_ref, table_ref, out_ref):
    planes, _, cells = u_ref.shape
    first = pl.program_id(0) * planes
    parts = [split(u_ref[k]) for k in range(planes)]
    high, low = (jnp.concatenate(values, axis=1) for values in zip(*parts))
    result = wide_dot(table_ref[...], high, low)
    stride = out_ref.shape[0] // POINTS
    for k in range(planes):
        out_ref[pl.ds(first + k, POINTS, stride=stride), :] = result[
            :, k * cells : (k + 1) * cells
        ]


def backward_kernel(w_ref, local_ref, table_ref, out_ref):
    planes, _, cells = out_ref.shape
    first = pl.program_id(0) * planes
    stride = w_ref.shape[0] // POINTS
    parts = [
        split(w_ref[pl.ds(first + k, POINTS, stride=stride), :]) for k in range(planes)
    ]
    high, low = (jnp.concatenate(values, axis=1) for values in zip(*parts))
    result = wide_dot(table_ref[...], high, low)
    for k in range(planes):
        out_ref[k] = result[:, k * cells : (k + 1) * cells] + local_ref[first + k]


def local_kernel(u_ref, friction_ref, shift_ref, out_ref):
    planes, _, cells = u_ref.shape
    for k in range(planes):
        high, low = split(u_ref[k])
        friction = dot(friction_ref[...], jnp.concatenate([high, low], axis=0))
        both = jnp.concatenate([high, low], axis=1)
        for side in range(2):
            part = slice(side * HALF, (side + 1) * HALF)
            moved = dot(both[part], shift_ref[side])
            out_ref[k, part, :] = friction[part] - moved * speed_over_60(
                side * HALF, HALF, cells
            )


def lane_select(values, lane, width):
    result = values[0]
    for index, value in enumerate(values[1:], 1):
        result = jnp.where(lane >= index * width, value, result)
    return result


def turn(value, shift):
    shift %= value.shape[1]
    return pltpu.roll(value, shift, 1) if shift else value


def pack(r_ref, near, far, side):
    cells = r_ref.shape[3]
    lane = lax.broadcasted_iota(jnp.int32, (POINTS, cells), 1)
    columns = [r_ref[:, q].reshape(POINTS, cells) for q in range(4)]
    wide_part = lane_select(
        [turn(v, 2 * NY * q - near) for q, v in enumerate(columns)], lane, 2 * NY
    )
    quarter = HALF // 2
    lane = lane[:quarter]
    thin_part = lane_select(
        [
            turn(columns[q][side * HALF + h * quarter : side * HALF + (h + 1) * quarter], NY * (q + 4 * h) - far)
            for h in range(2)
            for q in range(4)
        ],
        lane,
        NY,
    )
    return wide_part, thin_part


def halo_kernel(odd_ref, r_ref, first_ref, second_ref):
    owners = r_ref.shape[0] // 2
    cells = r_ref.shape[3]
    odd = odd_ref[0] == 1
    up = pack(r_ref.at[owners:], cells - 2 * NY, cells - 3 * NY, 1)
    down = pack(r_ref.at[:owners], 0, 2 * NY, 0)
    at = 0
    for upper, lower in zip(up, down):
        rows = upper.shape[0]
        first_ref[at : at + rows, :] = jnp.where(odd, lower, upper)
        second_ref[at : at + rows, :] = jnp.where(odd, upper, lower)
        at += rows


def load_columns(r_ref, x_ref):
    owners = r_ref.shape[0] // 2
    cells = r_ref.shape[3]
    for q in range(4):
        for side in range(2):
            value = r_ref[side * owners : (side + 1) * owners, q].reshape(POINTS, cells)
            high, low = split(value)
            at = (2 * q + side) * cells
            x_ref[0:POINTS, at : at + cells] = high
            x_ref[POINTS : 2 * POINTS, at : at + cells] = low


def middle_kernel(damp_ref, r_ref, forward_ref, symbol_ref, inverse_ref, inner_ref, out_ref, x_ref, y_ref):
    load_columns(r_ref, x_ref)
    spectrum = wide_dot(forward_ref[...], x_ref[0:POINTS, :], x_ref[POINTS:, :])
    width = spectrum.shape[1] // 4
    row = lax.broadcasted_iota(jnp.int32, (HALF, width), 0)
    scale = DAMPING / (HALF * HALF)
    damp_real = scale * (row * row).astype(F32)
    row_imag = jnp.where(row == 0, HALF, row)
    damp_imag = scale * (row_imag * row_imag).astype(F32)
    for slot in range(2):
        qa, qb = 2 * slot, 2 * slot + 1
        real_a, imag_a = (
            spectrum[h * HALF : (h + 1) * HALF, qa * width : (qa + 1) * width]
            for h in range(2)
        )
        real_b, imag_b = (
            spectrum[h * HALF : (h + 1) * HALF, qb * width : (qb + 1) * width]
            for h in range(2)
        )
        odd_a, odd_b = symbol_ref[slot, 0], symbol_ref[slot, 1]
        even_real, even_imag = symbol_ref[slot, 2], symbol_ref[slot, 3]
        da, db = damp_ref[qa], damp_ref[qb]
        results = (
            (qa, 0, -odd_a * imag_a - even_real * real_b - (damp_real + da) * real_a),
            (qa, 1, odd_a * real_a - even_imag * imag_b - (damp_imag + da) * imag_a),
            (qb, 0, -odd_b * imag_b + even_real * real_a - (damp_real + db) * real_b),
            (qb, 1, odd_b * real_b + even_imag * imag_a - (damp_imag + db) * imag_b),
        )
        for q, half, value in results:
            high, low = split(value)
            at = q * width
            y_ref[half * HALF : (half + 1) * HALF, at : at + width] = high
            y_ref[POINTS + half * HALF : POINTS + (half + 1) * HALF, at : at + width] = low
    cells = width // 2
    owners = out_ref.shape[0] // 2
    inverse = inverse_ref[...]
    friction = inverse[:, 2 * POINTS :]
    result = (
        wide_dot(inverse, y_ref[0:POINTS, :], y_ref[POINTS:, :])
        + dot(friction, x_ref[0:POINTS, :])
        + dot(friction, x_ref[POINTS:, :])
    )
    for side in range(2):
        part = slice(side * HALF, (side + 1) * HALF)
        low_part = slice(POINTS + side * HALF, POINTS + (side + 1) * HALF)
        moved = sum(
            dot(
                jnp.concatenate(
                    [x_ref[rows, q * width : (q + 1) * width] for q in range(4)], axis=0
                ),
                inner_ref[side],
            )
            for rows in (part, low_part)
        )
        speed = speed_over_60(side * HALF, HALF, width)
        rows = owners // 2
        for q in range(4):
            value = (
                result[part, q * width : (q + 1) * width]
                - moved[q * HALF : (q + 1) * HALF] * speed
            )
            for band in range(2):
                out_ref[
                    band * owners + side * rows : band * owners + (side + 1) * rows, q
                ] = value[:, band * cells : (band + 1) * cells].reshape(rows, -1, cells)


def lane_weight(lane, first_row, last_row, weight):
    return jnp.where((lane >= first_row * NY) & (lane < last_row * NY), weight, 0.0)


def edge_kernel(odd_ref, partial_ref, first_ref, second_ref, out_ref):
    for step in range(4):
        pl.when(pl.program_id(0) == step)(
            lambda step=step: edge_part(
                step // 2, step % 2, odd_ref, partial_ref, first_ref, second_ref, out_ref
            )
        )


def edge_part(band, side, odd_ref, partial_ref, first_ref, second_ref, out_ref):
    owners, _, _, cells = out_ref.shape
    band_rows = cells // NY
    stencil = dict((PLUS, MINUS)[side])
    weights = [stencil.get(s if band else -s) for s in (1, 2, 3)]
    odd = (odd_ref[0] == 1) != bool(band)
    lane = lax.broadcasted_iota(jnp.int32, (HALF, cells), 1)

    def received(rows):
        return jnp.where(odd, first_ref[rows, :], second_ref[rows, :])

    pair = received(slice(side * HALF, (side + 1) * HALF))
    thin = received(slice(POINTS, POINTS + HALF // 2)) if weights[2] else None
    speed = speed_over_60(side * HALF, HALF, cells)
    block = slice((2 * band + side) * owners, (2 * band + side + 1) * owners)
    for q in range(4):
        moved = 0.0
        for s, weight in enumerate(weights, 1):
            if weight is None:
                continue
            if band:
                near = band_rows - s
                rows = (near, min(near + 2, band_rows))
            else:
                near = s - 2
                rows = (max(near, 0), s)
            moved += lane_weight(lane, *rows, weight) * turn(pair, NY * (near - 2 * q))
        if thin is not None:
            row = band_rows - 1 if band else 0
            third = jnp.concatenate(
                [turn(thin, NY * (row - q - 4 * h)) for h in range(2)], axis=0
            )
            moved += lane_weight(lane, row, row + 1, weights[2]) * third
        out_ref[:, q] = partial_ref[block, q] - (moved * speed).reshape(owners, -1, cells)


VMEM_SPEC = pl.BlockSpec(memory_space=pltpu.VMEM)
SMEM_SPEC = pl.BlockSpec(memory_space=pltpu.SMEM)


def on_chip(value):
    return pltpu.with_memory_space_constraint(value, pltpu.VMEM)


def call(
    kernel,
    shapes,
    inputs,
    scratch=(),
    flops=1,
    smem=0,
    keep=True,
    grid=(),
    in_specs=None,
    out_specs=None,
):
    bytes_accessed = sum(v.size * v.dtype.itemsize for v in inputs)
    shapes = [pltpu.VMEM(*s) if keep else jax.ShapeDtypeStruct(*s) for s in shapes]
    if in_specs is None:
        inputs = [*inputs[:smem], *(on_chip(v) for v in inputs[smem:])]
        in_specs = [SMEM_SPEC] * smem + [VMEM_SPEC] * (len(inputs) - smem)
    if out_specs is None:
        out_specs = [VMEM_SPEC] * len(shapes)
    single = len(shapes) == 1
    return pl.pallas_call(
        kernel,
        grid=grid,
        out_shape=shapes[0] if single else shapes,
        in_specs=in_specs,
        out_specs=out_specs[0] if single else out_specs,
        scratch_shapes=list(scratch),
        cost_estimate=pl.CostEstimate(
            flops=flops, bytes_accessed=2 * bytes_accessed, transcendentals=0
        ),
        compiler_params=pltpu.CompilerParams(vmem_limit_bytes=24 << 20),
    )(*inputs)


def symbol_table(mode_waves, mode_amplitudes, mode_phases, first_slot, first_row, rows, total_rows):
    local = jnp.arange(rows * NY, dtype=jnp.int32)
    row, column = first_row + local // NY, local % NY
    turn_rows = mode_waves[:, 0:1] * row[None, :] % total_rows
    turn_columns = mode_waves[:, 1:2] * column[None, :] % NY
    angles = (
        2.0
        * math.pi
        * (turn_rows.astype(F32) / total_rows + turn_columns.astype(F32) / NY)
        + mode_phases[:, None]
    )
    cell_factor = mode_amplitudes[:, None] * jnp.sin(angles)
    scale = math.pi / POINTS

    def turned(waves, frequency):
        return scale * (waves * frequency % (2 * POINTS)).astype(F32)

    first_waves, second_waves = mode_waves[None, :, 0], mode_waves[None, :, 1]
    real_freq = jnp.arange(HALF, dtype=jnp.int32)[:, None]
    imag_freq = jnp.where(real_freq == 0, HALF, real_freq)
    odd_first = jnp.sin(turned(first_waves, real_freq))
    even_real = jnp.cos(turned(first_waves, real_freq))
    even_imag = jnp.cos(turned(first_waves, imag_freq))
    slots = first_slot + jnp.arange(2, dtype=jnp.int32)[:, None]
    slots_b = jnp.where(slots == 0, HALF, slots)
    odd_second = jnp.sin(turned(second_waves, slots))
    even_a = jnp.cos(turned(second_waves, slots))
    even_b = jnp.cos(turned(second_waves, slots_b))
    factors = jnp.stack(
        [
            odd_first[None] * even_a[:, None],
            odd_first[None] * even_b[:, None],
            even_real[None] * odd_second[:, None],
            even_imag[None] * odd_second[:, None],
        ],
        axis=1,
    )
    symbol = jnp.dot(
        factors.reshape(8 * HALF, -1), cell_factor, precision=HIGHEST_PRECISION
    ).reshape(2, 4, HALF, rows * NY)
    damp = DAMPING / (HALF * HALF) * jnp.stack(
        [slots * slots, slots_b * slots_b], axis=1
    ).reshape(4).astype(F32)
    return symbol, damp


def off_chip(value):
    return pltpu.with_memory_space_constraint(value, pltpu.HBM)


def stage_forward(density, table):
    planes, points, cells = density.shape
    sent = call(
        forward_kernel,
        [((points * planes, cells), F32)],
        (off_chip(density), off_chip(table["forward_second"])),
        flops=6 * points * points * planes * cells,
        keep=False,
        grid=(FORWARD_STEPS,),
        in_specs=[
            pl.BlockSpec((planes // FORWARD_STEPS, points, cells), lambda i: (i, 0, 0)),
            pl.BlockSpec((points, 2 * points), lambda i: (0, 0)),
        ],
        out_specs=[pl.BlockSpec((points * planes, cells), lambda i: (0, 0))],
    )
    return sent.reshape(points // 4, 4, planes, cells)


def stage_local(density, table):
    planes, points, cells = density.shape
    return call(
        local_kernel,
        [((planes, points, cells), F32)],
        (density, table["friction"], table["column_shift"]),
        flops=6 * points * points * planes * cells,
    )


def stage_halo(odd, columns):
    cells = columns.shape[3]
    return call(
        halo_kernel, [((POINTS + POINTS // 4, cells), F32)] * 2, (odd, columns), smem=1
    )


def stage_middle(damp, columns, symbol, table):
    _, _, _, cells = columns.shape
    width = 8 * cells
    scratch = pltpu.VMEM((2 * POINTS, width), BF16)
    return call(
        middle_kernel,
        [(columns.shape, F32)],
        (
            damp,
            columns,
            table["forward_first"],
            symbol,
            table["inverse_first"],
            table["row_inner"],
        ),
        (scratch, scratch),
        20 * POINTS * POINTS * width,
        smem=1,
    )


def stage_edge(odd, partial, first, second):
    members, _, planes, cells = partial.shape
    return call(
        edge_kernel,
        [(partial.shape, F32)],
        (odd, on_chip(partial), on_chip(first), on_chip(second)),
        flops=40 * partial.size,
        keep=False,
        grid=(4,),
        in_specs=[SMEM_SPEC] + [VMEM_SPEC] * 3,
        out_specs=[pl.BlockSpec((members // 4, 4, planes, cells), lambda i: (i, 0, 0, 0))],
    )


def stage_backward(panels, here, table):
    planes, points, cells = here.shape
    return call(
        backward_kernel,
        [((planes, points, cells), F32)],
        (
            on_chip(panels.reshape(points * planes, cells)),
            on_chip(here),
            on_chip(table["inverse_second"]),
        ),
        flops=6 * points * points * planes * cells,
        keep=False,
        grid=(BACKWARD_STEPS,),
        in_specs=[VMEM_SPEC] * 3,
        out_specs=[
            pl.BlockSpec((planes // BACKWARD_STEPS, points, cells), lambda i: (i, 0, 0))
        ],
    )


def local(density, mode_waves, mode_amplitudes, mode_phases):
    _, _, cells = density.shape
    rows_dev = cells // NY
    group = ("pair", "mom")
    strips = lax.axis_size("y")
    table = tables(rows_dev)

    sent = stage_forward(density, table)
    columns = lax.all_to_all(sent, group, split_axis=0, concat_axis=0, tiled=True)
    here = stage_local(density, table)
    position = lax.axis_index("pair") * lax.axis_size("mom") + lax.axis_index("mom")
    odd = (lax.axis_index("y") % 2).reshape(1)
    symbol, damp = symbol_table(
        mode_waves,
        mode_amplitudes,
        mode_phases,
        2 * position,
        lax.axis_index("y") * (2 * rows_dev),
        2 * rows_dev,
        2 * rows_dev * strips,
    )
    first, second = stage_halo(odd, columns)
    links = [(i, (i + 1) % strips) for i in range(strips)]
    swaps = [[p for l in links[start::2] for p in (l, l[::-1])] for start in range(2)]
    first = lax.ppermute(first, "y", swaps[0])
    second = lax.ppermute(second, "y", swaps[1])
    partial = stage_middle(damp, columns, symbol, table)
    back = stage_edge(odd, partial, first, second)
    panels = lax.all_to_all(back, group, split_axis=0, concat_axis=0, tiled=True)
    return stage_backward(panels, here, table)


def solution(mesh):
    bands = mesh.shape["space"]
    finer = jax.sharding.Mesh(
        mesh.devices.reshape(bands // 2, 2, mesh.shape["mom"]), ("y", "pair", "mom")
    )
    return jax.shard_map(
        local,
        mesh=finer,
        in_specs=(P("mom", None, ("y", "pair")), P(), P(), P()),
        out_specs=P("mom", None, ("y", "pair")),
        check_vma=False,
    )
```

```python
import math

import jax
import jax.numpy as jnp
import ml_dtypes
import numpy as np
from jax import lax
from jax.experimental import pallas as pl
from jax.experimental.pallas import tpu as pltpu
from jax.sharding import PartitionSpec as P

NY = 16
POINTS = 256
HALF = POINTS // 2
DAMPING = 0.5
FRICTION = 0.5
MINUS = ((-3, -2.0), (-2, 15.0), (-1, -60.0), (0, 20.0), (1, 30.0), (2, -3.0))
PLUS = ((3, 2.0), (2, -15.0), (1, 60.0), (0, -20.0), (-1, -30.0), (-2, 3.0))
F32 = jnp.float32
BF16 = jnp.bfloat16
HIGHEST_PRECISION = lax.Precision.HIGHEST
FORWARD_STEPS = 4
BACKWARD_STEPS = 2
LOCAL_STEPS = 2


def wide(table):
    high = table.astype(ml_dtypes.bfloat16)
    low = (table - high.astype(np.float64)).astype(ml_dtypes.bfloat16)
    return np.concatenate([high, low], axis=1)


def real_fourier():
    k = np.arange(POINTS)
    m = np.arange(HALF)
    angles = 2.0 * np.pi / POINTS * (m[:, None] * k[None, :] % POINTS)
    cosine, sine = np.cos(angles), -np.sin(angles)
    sine[0] = 1.0 - 2.0 * (k % 2)
    forward = np.concatenate([cosine, sine], axis=0)
    weight = np.full((HALF,), 2.0)
    weight[0] = 1.0
    inverse = (forward * np.concatenate([weight, weight])[:, None] / POINTS).T
    return forward, inverse


def interleaved(rows):
    return np.stack([rows[:HALF], rows[HALF:]], axis=1).reshape(POINTS, -1)


def friction_matrix():
    speed = (2.0 * np.arange(POINTS) - POINTS + 1) / POINTS
    result = np.zeros((POINTS, POINTS))
    k = np.arange(POINTS - 1)
    result[k, k + 1] = FRICTION * speed[k + 1]
    result[k + 1, k] = -FRICTION * speed[k]
    return result


def row_matrix(stencil, rows):
    result = np.zeros((rows * NY, rows * NY))
    for out_row in range(rows):
        for offset, weight in stencil:
            row = out_row + offset
            if 0 <= row < rows:
                for column in range(NY):
                    result[row * NY + column, out_row * NY + column] = weight
    return result


def column_matrix(stencil, rows):
    result = np.zeros((rows * NY, rows * NY))
    for row in range(rows):
        for column in range(NY):
            for offset, weight in stencil:
                result[row * NY + (column + offset) % NY, row * NY + column] += weight
    return result


def bf16_table(table):
    return jnp.asarray(table.astype(ml_dtypes.bfloat16))


def tables(rows_dev):
    forward, inverse = real_fourier()
    result = {}
    result["forward_second"] = jnp.asarray(wide(interleaved(forward)))
    result["inverse_second"] = jnp.asarray(wide(interleaved(inverse.T).T))
    result["forward_first"] = jnp.asarray(wide(forward))
    friction = friction_matrix().astype(ml_dtypes.bfloat16)
    result["inverse_first"] = jnp.asarray(wide(inverse))
    result["friction"] = jnp.asarray(np.concatenate([friction, friction], axis=1))
    rows = 2 * rows_dev
    result["row_inner"] = bf16_table(
        np.stack([row_matrix(stencil, rows) for stencil in (PLUS, MINUS)])
    )
    result["column_shift"] = bf16_table(
        np.stack(
            [
                np.concatenate([column_matrix(s, rows_dev)] * 2, axis=0)
                for s in (PLUS, MINUS)
            ]
        )
    )
    return result


def split(value):
    high = value.astype(BF16)
    low = (value - high.astype(F32)).astype(BF16)
    return high, low


def dot(left, right):
    return jnp.dot(left, right, preferred_element_type=F32)


def wide_dot(table, high, low):
    return (
        dot(table[:, :POINTS], high)
        + dot(table[:, :POINTS], low)
        + dot(table[:, POINTS : 2 * POINTS], high)
    )


def speed_over_60(first, count, width):
    index = first + lax.broadcasted_iota(jnp.int32, (count, width), 0)
    return (2 * index - (POINTS - 1)).astype(F32) * (1.0 / (60 * POINTS))


def forward_kernel(u_hbm, table_hbm, out_ref, u_ref, table_ref, sems):
    planes, _, cells = u_ref.shape
    step = planes // FORWARD_STEPS
    table_copy = pltpu.make_async_copy(table_hbm, table_ref, sems.at[FORWARD_STEPS])
    copies = [
        pltpu.make_async_copy(
            u_hbm.at[pl.ds(i * step, step)], u_ref.at[pl.ds(i * step, step)], sems.at[i]
        )
        for i in range(FORWARD_STEPS)
    ]
    copies[0].start()
    table_copy.start()
    for copy in copies[1:]:
        copy.start()
    for i, copy in enumerate(copies):
        copy.wait()
        if i == 0:
            table_copy.wait()
        parts = [split(u_ref[k]) for k in range(i * step, (i + 1) * step)]
        high, low = (jnp.concatenate(values, axis=1) for values in zip(*parts))
        result = wide_dot(table_ref[...], high, low)
        for k in range(step):
            out_ref[pl.ds(i * step + k, POINTS, stride=planes), :] = result[
                :, k * cells : (k + 1) * cells
            ]


def backward_kernel(w_ref, local_ref, table_ref, out_ref):
    planes, _, cells = out_ref.shape
    first = pl.program_id(0) * planes
    stride = w_ref.shape[0] // POINTS
    parts = [
        split(w_ref[pl.ds(first + k, POINTS, stride=stride), :]) for k in range(planes)
    ]
    high, low = (jnp.concatenate(values, axis=1) for values in zip(*parts))
    result = wide_dot(table_ref[...], high, low)
    for k in range(planes):
        out_ref[k] = result[:, k * cells : (k + 1) * cells] + local_ref[first + k]


def local_kernel(u_ref, friction_ref, shift_ref, out_ref):
    planes, _, cells = u_ref.shape
    first = pl.program_id(0) * planes
    for k in range(planes):
        high, low = split(u_ref[k])
        friction = dot(friction_ref[...], jnp.concatenate([high, low], axis=0))
        both = jnp.concatenate([high, low], axis=1)
        for side in range(2):
            part = slice(side * HALF, (side + 1) * HALF)
            moved = dot(both[part], shift_ref[side])
            out_ref[first + k, part, :] = friction[part] - moved * speed_over_60(
                side * HALF, HALF, cells
            )


def lane_select(values, lane, width):
    result = values[0]
    for index, value in enumerate(values[1:], 1):
        result = jnp.where(lane >= index * width, value, result)
    return result


def turn(value, shift):
    shift %= value.shape[1]
    return pltpu.roll(value, shift, 1) if shift else value


def pack(r_ref, near, far, side):
    cells = r_ref.shape[3]
    lane = lax.broadcasted_iota(jnp.int32, (POINTS, cells), 1)
    columns = [r_ref[:, q].reshape(POINTS, cells) for q in range(4)]
    wide_part = lane_select(
        [turn(v, 2 * NY * q - near) for q, v in enumerate(columns)], lane, 2 * NY
    )
    quarter = HALF // 2
    lane = lane[:quarter]
    thin_part = lane_select(
        [
            turn(columns[q][side * HALF + h * quarter : side * HALF + (h + 1) * quarter], NY * (q + 4 * h) - far)
            for h in range(2)
            for q in range(4)
        ],
        lane,
        NY,
    )
    return wide_part, thin_part


def halo_kernel(odd_ref, r_ref, first_ref, second_ref):
    owners = r_ref.shape[0] // 2
    cells = r_ref.shape[3]
    odd = odd_ref[0] == 1
    up = pack(r_ref.at[owners:], cells - 2 * NY, cells - 3 * NY, 1)
    down = pack(r_ref.at[:owners], 0, 2 * NY, 0)
    at = 0
    for upper, lower in zip(up, down):
        rows = upper.shape[0]
        first_ref[at : at + rows, :] = jnp.where(odd, lower, upper)
        second_ref[at : at + rows, :] = jnp.where(odd, upper, lower)
        at += rows


def load_columns(r_ref, x_ref):
    owners = r_ref.shape[0] // 2
    cells = r_ref.shape[3]
    for q in range(4):
        for side in range(2):
            value = r_ref[side * owners : (side + 1) * owners, q].reshape(POINTS, cells)
            high, low = split(value)
            at = (2 * q + side) * cells
            x_ref[0:POINTS, at : at + cells] = high
            x_ref[POINTS : 2 * POINTS, at : at + cells] = low


def first_friction(value):
    index = lax.broadcasted_iota(jnp.int32, value.shape, 0)
    weighted = value * (
        (2 * index - (POINTS - 1)).astype(F32) * (FRICTION / POINTS)
    )
    later = jnp.where(index < POINTS - 1, pltpu.roll(weighted, POINTS - 1, 0), 0.0)
    earlier = jnp.where(index > 0, pltpu.roll(weighted, 1, 0), 0.0)
    return later - earlier


def middle_kernel(
    damp_ref, r_ref, forward_ref, symbol_ref, inverse_ref, inner_hbm, out_ref, x_ref, y_ref, inner_ref, sem
):
    inner_copy = pltpu.make_async_copy(inner_hbm, inner_ref, sem)
    inner_copy.start()
    load_columns(r_ref, x_ref)
    spectrum = wide_dot(forward_ref[...], x_ref[0:POINTS, :], x_ref[POINTS:, :])
    width = spectrum.shape[1] // 4
    row = lax.broadcasted_iota(jnp.int32, (HALF, width), 0)
    scale = DAMPING / (HALF * HALF)
    damp_real = scale * (row * row).astype(F32)
    row_imag = jnp.where(row == 0, HALF, row)
    damp_imag = scale * (row_imag * row_imag).astype(F32)
    for slot in range(2):
        qa, qb = 2 * slot, 2 * slot + 1
        real_a, imag_a = (
            spectrum[h * HALF : (h + 1) * HALF, qa * width : (qa + 1) * width]
            for h in range(2)
        )
        real_b, imag_b = (
            spectrum[h * HALF : (h + 1) * HALF, qb * width : (qb + 1) * width]
            for h in range(2)
        )
        odd_a, odd_b = symbol_ref[slot, 0], symbol_ref[slot, 1]
        even_real, even_imag = symbol_ref[slot, 2], symbol_ref[slot, 3]
        da, db = damp_ref[qa], damp_ref[qb]
        results = (
            (qa, 0, -odd_a * imag_a - even_real * real_b - (damp_real + da) * real_a),
            (qa, 1, odd_a * real_a - even_imag * imag_b - (damp_imag + da) * imag_a),
            (qb, 0, -odd_b * imag_b + even_real * real_a - (damp_real + db) * real_b),
            (qb, 1, odd_b * real_b + even_imag * imag_a - (damp_imag + db) * imag_b),
        )
        for q, half, value in results:
            high, low = split(value)
            at = q * width
            y_ref[half * HALF : (half + 1) * HALF, at : at + width] = high
            y_ref[POINTS + half * HALF : POINTS + (half + 1) * HALF, at : at + width] = low
    cells = width // 2
    owners = out_ref.shape[0] // 2
    result = wide_dot(inverse_ref[...], y_ref[0:POINTS, :], y_ref[POINTS:, :])
    inner_copy.wait()
    moved = [
        sum(
            dot(
                jnp.concatenate(
                    [
                        x_ref[
                            half + side * HALF : half + (side + 1) * HALF,
                            q * width : (q + 1) * width,
                        ]
                        for q in range(4)
                    ],
                    axis=0,
                ),
                inner_ref[side],
            )
            for half in (0, POINTS)
        )
        for side in range(2)
    ]
    rows = owners // 2
    for q in range(4):
        for band in range(2):
            here = r_ref[band * owners : (band + 1) * owners, q].reshape(POINTS, cells)
            friction = first_friction(here)
            inside = slice(band * cells, (band + 1) * cells)
            for side in range(2):
                part = slice(side * HALF, (side + 1) * HALF)
                value = (
                    result[part, q * width : (q + 1) * width][:, inside]
                    + friction[part]
                    - moved[side][q * HALF : (q + 1) * HALF, inside]
                    * speed_over_60(side * HALF, HALF, cells)
                )
                at = band * owners + side * rows
                out_ref[at : at + rows, q] = value.reshape(rows, -1, cells)


def lane_weight(lane, first_row, last_row, weight):
    return jnp.where((lane >= first_row * NY) & (lane < last_row * NY), weight, 0.0)


def edge_kernel(odd_ref, partial_ref, first_ref, second_ref, out_ref):
    for step in range(4):
        edge_part(
            step // 2, step % 2, odd_ref, partial_ref, first_ref, second_ref, out_ref
        )


def edge_part(band, side, odd_ref, partial_ref, first_ref, second_ref, out_ref):
    members, _, _, cells = out_ref.shape
    owners = members // 4
    band_rows = cells // NY
    stencil = dict((PLUS, MINUS)[side])
    weights = [stencil.get(s if band else -s) for s in (1, 2, 3)]
    odd = (odd_ref[0] == 1) != bool(band)
    lane = lax.broadcasted_iota(jnp.int32, (HALF, cells), 1)

    def received(rows):
        return jnp.where(odd, first_ref[rows, :], second_ref[rows, :])

    pair = received(slice(side * HALF, (side + 1) * HALF))
    thin = received(slice(POINTS, POINTS + HALF // 2)) if weights[2] else None
    speed = speed_over_60(side * HALF, HALF, cells)
    block = slice((2 * band + side) * owners, (2 * band + side + 1) * owners)
    for q in range(4):
        moved = 0.0
        for s, weight in enumerate(weights, 1):
            if weight is None:
                continue
            if band:
                near = band_rows - s
                rows = (near, min(near + 2, band_rows))
            else:
                near = s - 2
                rows = (max(near, 0), s)
            moved += lane_weight(lane, *rows, weight) * turn(pair, NY * (near - 2 * q))
        if thin is not None:
            row = band_rows - 1 if band else 0
            third = jnp.concatenate(
                [turn(thin, NY * (row - q - 4 * h)) for h in range(2)], axis=0
            )
            moved += lane_weight(lane, row, row + 1, weights[2]) * third
        out_ref[block, q] = partial_ref[block, q] - (moved * speed).reshape(owners, -1, cells)


VMEM_SPEC = pl.BlockSpec(memory_space=pltpu.VMEM)
SMEM_SPEC = pl.BlockSpec(memory_space=pltpu.SMEM)


def on_chip(value):
    return pltpu.with_memory_space_constraint(value, pltpu.VMEM)


def call(
    kernel,
    shapes,
    inputs,
    scratch=(),
    flops=1,
    smem=0,
    keep=True,
    grid=(),
    in_specs=None,
    out_specs=None,
):
    bytes_accessed = sum(v.size * v.dtype.itemsize for v in inputs)
    shapes = [pltpu.VMEM(*s) if keep else jax.ShapeDtypeStruct(*s) for s in shapes]
    if in_specs is None:
        inputs = [*inputs[:smem], *(on_chip(v) for v in inputs[smem:])]
        in_specs = [SMEM_SPEC] * smem + [VMEM_SPEC] * (len(inputs) - smem)
    if out_specs is None:
        out_specs = [VMEM_SPEC] * len(shapes)
    single = len(shapes) == 1
    return pl.pallas_call(
        kernel,
        grid=grid,
        out_shape=shapes[0] if single else shapes,
        in_specs=in_specs,
        out_specs=out_specs[0] if single else out_specs,
        scratch_shapes=list(scratch),
        cost_estimate=pl.CostEstimate(
            flops=flops, bytes_accessed=2 * bytes_accessed, transcendentals=0
        ),
        compiler_params=pltpu.CompilerParams(vmem_limit_bytes=24 << 20),
    )(*inputs)


def symbol_table(mode_waves, mode_amplitudes, mode_phases, first_slot, first_row, rows, total_rows):
    local = jnp.arange(rows * NY, dtype=jnp.int32)
    row, column = first_row + local // NY, local % NY
    turn_rows = mode_waves[:, 0:1] * row[None, :] % total_rows
    turn_columns = mode_waves[:, 1:2] * column[None, :] % NY
    angles = (
        2.0
        * math.pi
        * (turn_rows.astype(F32) / total_rows + turn_columns.astype(F32) / NY)
        + mode_phases[:, None]
    )
    cell_factor = mode_amplitudes[:, None] * jnp.sin(angles)
    scale = math.pi / POINTS

    def turned(waves, frequency):
        return scale * (waves * frequency % (2 * POINTS)).astype(F32)

    first_waves, second_waves = mode_waves[None, :, 0], mode_waves[None, :, 1]
    real_freq = jnp.arange(HALF, dtype=jnp.int32)[:, None]
    imag_freq = jnp.where(real_freq == 0, HALF, real_freq)
    odd_first = jnp.sin(turned(first_waves, real_freq))
    even_real = jnp.cos(turned(first_waves, real_freq))
    even_imag = jnp.cos(turned(first_waves, imag_freq))
    slots = first_slot + jnp.arange(2, dtype=jnp.int32)[:, None]
    slots_b = jnp.where(slots == 0, HALF, slots)
    odd_second = jnp.sin(turned(second_waves, slots))
    even_a = jnp.cos(turned(second_waves, slots))
    even_b = jnp.cos(turned(second_waves, slots_b))
    factors = jnp.stack(
        [
            odd_first[None] * even_a[:, None],
            odd_first[None] * even_b[:, None],
            even_real[None] * odd_second[:, None],
            even_imag[None] * odd_second[:, None],
        ],
        axis=1,
    )
    symbol = jnp.dot(
        factors.reshape(8 * HALF, -1), cell_factor, precision=HIGHEST_PRECISION
    ).reshape(2, 4, HALF, rows * NY)
    damp = DAMPING / (HALF * HALF) * jnp.stack(
        [slots * slots, slots_b * slots_b], axis=1
    ).reshape(4).astype(F32)
    return symbol, damp


def off_chip(value):
    return pltpu.with_memory_space_constraint(value, pltpu.HBM)


def stage_forward(density, table):
    planes, points, cells = density.shape
    sent = call(
        forward_kernel,
        [((points * planes, cells), F32)],
        (off_chip(density), off_chip(table["forward_second"])),
        (
            pltpu.VMEM(density.shape, F32),
            pltpu.VMEM((points, 2 * points), BF16),
            pltpu.SemaphoreType.DMA((FORWARD_STEPS + 1,)),
        ),
        flops=6 * points * points * planes * cells,
        keep=False,
        in_specs=[pl.BlockSpec(memory_space=pl.ANY)] * 2,
    )
    return sent.reshape(points // 4, 4, planes, cells)


def stage_local(density, table):
    planes, points, cells = density.shape
    friction, shift = table["friction"], table["column_shift"]
    return call(
        local_kernel,
        [((planes, points, cells), F32)],
        (off_chip(density), off_chip(friction), off_chip(shift)),
        flops=6 * points * points * planes * cells,
        grid=(LOCAL_STEPS,),
        in_specs=[
            pl.BlockSpec((planes // LOCAL_STEPS, points, cells), lambda i: (i, 0, 0)),
            pl.BlockSpec(friction.shape, lambda i: (0, 0)),
            pl.BlockSpec(shift.shape, lambda i: (0, 0, 0)),
        ],
    )


def stage_halo(odd, columns):
    cells = columns.shape[3]
    return call(
        halo_kernel, [((POINTS + POINTS // 4, cells), F32)] * 2, (odd, columns), smem=1
    )


def stage_middle(damp, columns, symbol, table):
    _, _, _, cells = columns.shape
    width = 8 * cells
    inner = table["row_inner"]
    scratch = pltpu.VMEM((2 * POINTS, width), BF16)
    return call(
        middle_kernel,
        [(columns.shape, F32)],
        (
            damp,
            on_chip(columns),
            on_chip(table["forward_first"]),
            on_chip(symbol),
            on_chip(table["inverse_first"]),
            off_chip(inner),
        ),
        (scratch, scratch, pltpu.VMEM(inner.shape, BF16), pltpu.SemaphoreType.DMA),
        20 * POINTS * POINTS * width,
        in_specs=[SMEM_SPEC] + [VMEM_SPEC] * 4 + [pl.BlockSpec(memory_space=pl.ANY)],
    )


def stage_edge(odd, partial, first, second):
    return call(
        edge_kernel,
        [(partial.shape, F32)],
        (odd, partial, first, second),
        flops=40 * partial.size,
        smem=1,
        keep=False,
    )


def stage_backward(panels, here, table):
    planes, points, cells = here.shape
    return call(
        backward_kernel,
        [((planes, points, cells), F32)],
        (
            on_chip(panels.reshape(points * planes, cells)),
            on_chip(here),
            on_chip(table["inverse_second"]),
        ),
        flops=6 * points * points * planes * cells,
        keep=False,
        grid=(BACKWARD_STEPS,),
        in_specs=[VMEM_SPEC] * 3,
        out_specs=[
            pl.BlockSpec((planes // BACKWARD_STEPS, points, cells), lambda i: (i, 0, 0))
        ],
    )


def local(density, mode_waves, mode_amplitudes, mode_phases):
    _, _, cells = density.shape
    rows_dev = cells // NY
    group = ("pair", "mom")
    strips = lax.axis_size("y")
    table = tables(rows_dev)

    sent = stage_forward(density, table)
    columns = lax.all_to_all(sent, group, split_axis=0, concat_axis=0, tiled=True)
    here = stage_local(density, table)
    position = lax.axis_index("pair") * lax.axis_size("mom") + lax.axis_index("mom")
    odd = (lax.axis_index("y") % 2).reshape(1)
    symbol, damp = symbol_table(
        mode_waves,
        mode_amplitudes,
        mode_phases,
        2 * position,
        lax.axis_index("y") * (2 * rows_dev),
        2 * rows_dev,
        2 * rows_dev * strips,
    )
    first, second = stage_halo(odd, columns)
    links = [(i, (i + 1) % strips) for i in range(strips)]
    swaps = [[p for l in links[start::2] for p in (l, l[::-1])] for start in range(2)]
    first = lax.ppermute(first, "y", swaps[0])
    second = lax.ppermute(second, "y", swaps[1])
    partial = stage_middle(damp, columns, symbol, table)
    back = stage_edge(odd, partial, first, second)
    panels = lax.all_to_all(back, group, split_axis=0, concat_axis=0, tiled=True)
    return stage_backward(panels, here, table)


def solution(mesh):
    bands = mesh.shape["space"]
    finer = jax.sharding.Mesh(
        mesh.devices.reshape(bands // 2, 2, mesh.shape["mom"]), ("y", "pair", "mom")
    )
    return jax.shard_map(
        local,
        mesh=finer,
        in_specs=(P("mom", None, ("y", "pair")), P(), P(), P()),
        out_specs=P("mom", None, ("y", "pair")),
        check_vma=False,
    )
```

```python
import functools
import math

import jax
import jax.numpy as jnp
import ml_dtypes
import numpy as np
from jax import lax
from jax.experimental import pallas as pl
from jax.experimental.pallas import tpu as pltpu
from jax.sharding import PartitionSpec as P

NY = 16
POINTS = 256
HALF = POINTS // 2
DAMPING = 0.5
FRICTION = 0.5
MINUS = ((-3, -2.0), (-2, 15.0), (-1, -60.0), (0, 20.0), (1, 30.0), (2, -3.0))
PLUS = ((3, 2.0), (2, -15.0), (1, 60.0), (0, -20.0), (-1, -30.0), (-2, 3.0))
F32 = jnp.float32
BF16 = jnp.bfloat16
HIGHEST_PRECISION = lax.Precision.HIGHEST
FORWARD_STEPS = 1
BACKWARD_STEPS = 1
LOCAL_STEPS = 2


def wide(table):
    high = table.astype(ml_dtypes.bfloat16)
    low = (table - high.astype(np.float64)).astype(ml_dtypes.bfloat16)
    return np.concatenate([high, low], axis=1)


def real_fourier():
    k = np.arange(POINTS)
    m = np.arange(HALF)
    angles = 2.0 * np.pi / POINTS * (m[:, None] * k[None, :] % POINTS)
    cosine, sine = np.cos(angles), -np.sin(angles)
    sine[0] = 1.0 - 2.0 * (k % 2)
    forward = np.concatenate([cosine, sine], axis=0)
    weight = np.full((HALF,), 2.0)
    weight[0] = 1.0
    inverse = (forward * np.concatenate([weight, weight])[:, None] / POINTS).T
    return forward, inverse


def interleaved(rows):
    return np.stack([rows[:HALF], rows[HALF:]], axis=1).reshape(POINTS, -1)


def friction_matrix():
    speed = (2.0 * np.arange(POINTS) - POINTS + 1) / POINTS
    result = np.zeros((POINTS, POINTS))
    k = np.arange(POINTS - 1)
    result[k, k + 1] = FRICTION * speed[k + 1]
    result[k + 1, k] = -FRICTION * speed[k]
    return result


def row_matrix(stencil, rows):
    result = np.zeros((rows * NY, rows * NY))
    for out_row in range(rows):
        for offset, weight in stencil:
            row = out_row + offset
            if 0 <= row < rows:
                for column in range(NY):
                    result[row * NY + column, out_row * NY + column] = weight
    return result


def column_matrix(stencil, rows):
    result = np.zeros((rows * NY, rows * NY))
    for row in range(rows):
        for column in range(NY):
            for offset, weight in stencil:
                result[row * NY + (column + offset) % NY, row * NY + column] += weight
    return result


def bf16_table(table):
    return jnp.asarray(table.astype(ml_dtypes.bfloat16))


def tables(rows_dev):
    forward, inverse = real_fourier()
    result = {}
    result["forward_second"] = jnp.asarray(wide(interleaved(forward)))
    result["inverse_second"] = jnp.asarray(wide(interleaved(inverse.T).T))
    result["forward_first"] = jnp.asarray(wide(forward))
    friction = friction_matrix().astype(ml_dtypes.bfloat16)
    result["inverse_first"] = jnp.asarray(wide(inverse))
    result["friction"] = jnp.asarray(np.concatenate([friction, friction], axis=1))
    rows = 2 * rows_dev
    result["row_inner"] = bf16_table(
        np.stack([row_matrix(stencil, rows) for stencil in (PLUS, MINUS)])
    )
    result["column_shift"] = bf16_table(
        np.stack(
            [
                np.concatenate([column_matrix(s, rows_dev)] * 2, axis=0)
                for s in (PLUS, MINUS)
            ]
        )
    )
    return result


def split(value):
    high = value.astype(BF16)
    low = (value - high.astype(F32)).astype(BF16)
    return high, low


def dot(left, right):
    return jnp.dot(left, right, preferred_element_type=F32)


def wide_dot(table, high, low):
    return (
        dot(table[:, :POINTS], high)
        + dot(table[:, :POINTS], low)
        + dot(table[:, POINTS : 2 * POINTS], high)
    )


def speed_over_60(first, count, width):
    index = first + lax.broadcasted_iota(jnp.int32, (count, width), 0)
    return (2 * index - (POINTS - 1)).astype(F32) * (1.0 / (60 * POINTS))


def forward_kernel(u_hbm, table_hbm, out_ref, u_ref, table_ref, sems):
    planes, _, cells = u_ref.shape
    step = planes // FORWARD_STEPS
    table_copy = pltpu.make_async_copy(table_hbm, table_ref, sems.at[FORWARD_STEPS])
    copies = [
        pltpu.make_async_copy(
            u_hbm.at[pl.ds(i * step, step)], u_ref.at[pl.ds(i * step, step)], sems.at[i]
        )
        for i in range(FORWARD_STEPS)
    ]
    copies[0].start()
    table_copy.start()
    for copy in copies[1:]:
        copy.start()
    for i, copy in enumerate(copies):
        copy.wait()
        if i == 0:
            table_copy.wait()
        parts = [split(u_ref[k]) for k in range(i * step, (i + 1) * step)]
        high, low = (jnp.concatenate(values, axis=1) for values in zip(*parts))
        result = wide_dot(table_ref[...], high, low)
        for k in range(step):
            out_ref[pl.ds(i * step + k, POINTS, stride=planes), :] = result[
                :, k * cells : (k + 1) * cells
            ]


def backward_kernel(w_ref, local_ref, table_ref, out_ref):
    planes, _, cells = out_ref.shape
    first = pl.program_id(0) * planes
    stride = w_ref.shape[0] // POINTS
    parts = [
        split(w_ref[pl.ds(first + k, POINTS, stride=stride), :]) for k in range(planes)
    ]
    high, low = (jnp.concatenate(values, axis=1) for values in zip(*parts))
    result = wide_dot(table_ref[...], high, low)
    for k in range(planes):
        out_ref[k] = result[:, k * cells : (k + 1) * cells] + local_ref[first + k]


def local_kernel(u_ref, friction_ref, shift_ref, out_ref):
    planes, _, cells = u_ref.shape
    first = pl.program_id(0) * planes
    for k in range(planes):
        high, low = split(u_ref[k])
        friction = dot(friction_ref[...], jnp.concatenate([high, low], axis=0))
        both = jnp.concatenate([high, low], axis=1)
        for side in range(2):
            part = slice(side * HALF, (side + 1) * HALF)
            moved = dot(both[part], shift_ref[side])
            out_ref[first + k, part, :] = friction[part] - moved * speed_over_60(
                side * HALF, HALF, cells
            )


def lane_select(values, lane, width):
    result = values[0]
    for index, value in enumerate(values[1:], 1):
        result = jnp.where(lane >= index * width, value, result)
    return result


def turn(value, shift):
    shift %= value.shape[1]
    return pltpu.roll(value, shift, 1) if shift else value


def pack(r_ref, near, far, side):
    cells = r_ref.shape[3]
    lane = lax.broadcasted_iota(jnp.int32, (POINTS, cells), 1)
    columns = [r_ref[:, q].reshape(POINTS, cells) for q in range(4)]
    wide_part = lane_select(
        [turn(v, 2 * NY * q - near) for q, v in enumerate(columns)], lane, 2 * NY
    )
    quarter = HALF // 2
    lane = lane[:quarter]
    thin_part = lane_select(
        [
            turn(columns[q][side * HALF + h * quarter : side * HALF + (h + 1) * quarter], NY * (q + 4 * h) - far)
            for h in range(2)
            for q in range(4)
        ],
        lane,
        NY,
    )
    return wide_part, thin_part


def halo_kernel(odd_ref, r_ref, first_ref, second_ref):
    owners = r_ref.shape[0] // 2
    cells = r_ref.shape[3]
    odd = odd_ref[0] == 1
    up = pack(r_ref.at[owners:], cells - 2 * NY, cells - 3 * NY, 1)
    down = pack(r_ref.at[:owners], 0, 2 * NY, 0)
    at = 0
    for upper, lower in zip(up, down):
        rows = upper.shape[0]
        first_ref[at : at + rows, :] = jnp.where(odd, lower, upper)
        second_ref[at : at + rows, :] = jnp.where(odd, upper, lower)
        at += rows


def load_columns(r_ref, x_ref):
    owners = r_ref.shape[0] // 2
    cells = r_ref.shape[3]
    for q in range(4):
        for side in range(2):
            value = r_ref[side * owners : (side + 1) * owners, q].reshape(POINTS, cells)
            high, low = split(value)
            at = (2 * q + side) * cells
            x_ref[0:POINTS, at : at + cells] = high
            x_ref[POINTS : 2 * POINTS, at : at + cells] = low


def first_friction(value):
    index = lax.broadcasted_iota(jnp.int32, value.shape, 0)
    weighted = value * (
        (2 * index - (POINTS - 1)).astype(F32) * (FRICTION / POINTS)
    )
    later = jnp.where(index < POINTS - 1, pltpu.roll(weighted, POINTS - 1, 0), 0.0)
    earlier = jnp.where(index > 0, pltpu.roll(weighted, 1, 0), 0.0)
    return later - earlier


def middle_kernel(
    damp_ref, r_ref, forward_ref, symbol_ref, inverse_ref, inner_ref, out_ref, x_ref, y_ref
):
    load_columns(r_ref, x_ref)
    spectrum = wide_dot(forward_ref[...], x_ref[0:POINTS, :], x_ref[POINTS:, :])
    width = spectrum.shape[1] // 4
    row = lax.broadcasted_iota(jnp.int32, (HALF, width), 0)
    scale = DAMPING / (HALF * HALF)
    damp_real = scale * (row * row).astype(F32)
    row_imag = jnp.where(row == 0, HALF, row)
    damp_imag = scale * (row_imag * row_imag).astype(F32)
    for slot in range(2):
        qa, qb = 2 * slot, 2 * slot + 1
        real_a, imag_a = (
            spectrum[h * HALF : (h + 1) * HALF, qa * width : (qa + 1) * width]
            for h in range(2)
        )
        real_b, imag_b = (
            spectrum[h * HALF : (h + 1) * HALF, qb * width : (qb + 1) * width]
            for h in range(2)
        )
        odd_a, odd_b = symbol_ref[slot, 0], symbol_ref[slot, 1]
        even_real, even_imag = symbol_ref[slot, 2], symbol_ref[slot, 3]
        da, db = damp_ref[qa], damp_ref[qb]
        results = (
            (qa, 0, -odd_a * imag_a - even_real * real_b - (damp_real + da) * real_a),
            (qa, 1, odd_a * real_a - even_imag * imag_b - (damp_imag + da) * imag_a),
            (qb, 0, -odd_b * imag_b + even_real * real_a - (damp_real + db) * real_b),
            (qb, 1, odd_b * real_b + even_imag * imag_a - (damp_imag + db) * imag_b),
        )
        for q, half, value in results:
            high, low = split(value)
            at = q * width
            y_ref[half * HALF : (half + 1) * HALF, at : at + width] = high
            y_ref[POINTS + half * HALF : POINTS + (half + 1) * HALF, at : at + width] = low
    cells = width // 2
    owners = out_ref.shape[0] // 2
    result = wide_dot(inverse_ref[...], y_ref[0:POINTS, :], y_ref[POINTS:, :])
    moved = [
        sum(
            dot(
                jnp.concatenate(
                    [
                        x_ref[
                            half + side * HALF : half + (side + 1) * HALF,
                            q * width : (q + 1) * width,
                        ]
                        for q in range(4)
                    ],
                    axis=0,
                ),
                inner_ref[side],
            )
            for half in (0, POINTS)
        )
        for side in range(2)
    ]
    rows = owners // 2
    for q in range(4):
        for band in range(2):
            here = r_ref[band * owners : (band + 1) * owners, q].reshape(POINTS, cells)
            friction = first_friction(here)
            inside = slice(band * cells, (band + 1) * cells)
            for side in range(2):
                part = slice(side * HALF, (side + 1) * HALF)
                value = (
                    result[part, q * width : (q + 1) * width][:, inside]
                    + friction[part]
                    - moved[side][q * HALF : (q + 1) * HALF, inside]
                    * speed_over_60(side * HALF, HALF, cells)
                )
                at = band * owners + side * rows
                out_ref[at : at + rows, q] = value.reshape(rows, -1, cells)


def lane_weight(lane, first_row, last_row, weight):
    return jnp.where((lane >= first_row * NY) & (lane < last_row * NY), weight, 0.0)


def edge_kernel(odd_band, odd_ref, partial_ref, halo_ref, *refs):
    out_ref = refs[-1]
    for odd in range(2):

        @pl.when(odd_ref[0] == odd)
        def _(band=odd_band if odd else 1 - odd_band):
            for side in range(2):
                edge_part(band, side, partial_ref, halo_ref, out_ref)


def edge_part(band, side, partial_ref, halo_ref, out_ref):
    members, _, _, cells = out_ref.shape
    owners = members // 2
    band_rows = cells // NY
    stencil = dict((PLUS, MINUS)[side])
    weights = [stencil.get(s if band else -s) for s in (1, 2, 3)]
    lane = lax.broadcasted_iota(jnp.int32, (HALF, cells), 1)
    pair = halo_ref[side * HALF : (side + 1) * HALF, :]
    thin = halo_ref[POINTS : POINTS + HALF // 2, :]
    speed = speed_over_60(side * HALF, HALF, cells)
    here = slice(side * owners, (side + 1) * owners)
    block = slice((2 * band + side) * owners, (2 * band + side + 1) * owners)
    for q in range(4):
        moved = 0.0
        for s, weight in enumerate(weights, 1):
            if weight is None:
                continue
            if band:
                near = band_rows - s
                rows = (near, min(near + 2, band_rows))
            else:
                near = s - 2
                rows = (max(near, 0), s)
            moved += lane_weight(lane, *rows, weight) * turn(pair, NY * (near - 2 * q))
        if weights[2] is not None:
            row = band_rows - 1 if band else 0
            third = jnp.concatenate(
                [turn(thin, NY * (row - q - 4 * h)) for h in range(2)], axis=0
            )
            moved += lane_weight(lane, row, row + 1, weights[2]) * third
        out_ref[here, q] = partial_ref[block, q] - (moved * speed).reshape(owners, -1, cells)


VMEM_SPEC = pl.BlockSpec(memory_space=pltpu.VMEM)
SMEM_SPEC = pl.BlockSpec(memory_space=pltpu.SMEM)


def on_chip(value):
    return pltpu.with_memory_space_constraint(value, pltpu.VMEM)


def call(
    kernel,
    shapes,
    inputs,
    scratch=(),
    flops=1,
    smem=0,
    keep=True,
    grid=(),
    in_specs=None,
    out_specs=None,
):
    bytes_accessed = sum(v.size * v.dtype.itemsize for v in inputs)
    shapes = [pltpu.VMEM(*s) if keep else jax.ShapeDtypeStruct(*s) for s in shapes]
    if in_specs is None:
        inputs = [*inputs[:smem], *(on_chip(v) for v in inputs[smem:])]
        in_specs = [SMEM_SPEC] * smem + [VMEM_SPEC] * (len(inputs) - smem)
    if out_specs is None:
        out_specs = [VMEM_SPEC] * len(shapes)
    single = len(shapes) == 1
    return pl.pallas_call(
        kernel,
        grid=grid,
        out_shape=shapes[0] if single else shapes,
        in_specs=in_specs,
        out_specs=out_specs[0] if single else out_specs,
        scratch_shapes=list(scratch),
        cost_estimate=pl.CostEstimate(
            flops=flops, bytes_accessed=2 * bytes_accessed, transcendentals=0
        ),
        compiler_params=pltpu.CompilerParams(vmem_limit_bytes=24 << 20),
    )(*inputs)


def symbol_table(mode_waves, mode_amplitudes, mode_phases, first_slot, first_row, rows, total_rows):
    local = jnp.arange(rows * NY, dtype=jnp.int32)
    row, column = first_row + local // NY, local % NY
    turn_rows = mode_waves[:, 0:1] * row[None, :] % total_rows
    turn_columns = mode_waves[:, 1:2] * column[None, :] % NY
    angles = (
        2.0
        * math.pi
        * (turn_rows.astype(F32) / total_rows + turn_columns.astype(F32) / NY)
        + mode_phases[:, None]
    )
    cell_factor = mode_amplitudes[:, None] * jnp.sin(angles)
    scale = math.pi / POINTS

    def turned(waves, frequency):
        return scale * (waves * frequency % (2 * POINTS)).astype(F32)

    first_waves, second_waves = mode_waves[None, :, 0], mode_waves[None, :, 1]
    real_freq = jnp.arange(HALF, dtype=jnp.int32)[:, None]
    imag_freq = jnp.where(real_freq == 0, HALF, real_freq)
    odd_first = jnp.sin(turned(first_waves, real_freq))
    even_real = jnp.cos(turned(first_waves, real_freq))
    even_imag = jnp.cos(turned(first_waves, imag_freq))
    slots = first_slot + jnp.arange(2, dtype=jnp.int32)[:, None]
    slots_b = jnp.where(slots == 0, HALF, slots)
    odd_second = jnp.sin(turned(second_waves, slots))
    even_a = jnp.cos(turned(second_waves, slots))
    even_b = jnp.cos(turned(second_waves, slots_b))
    factors = jnp.stack(
        [
            odd_first[None] * even_a[:, None],
            odd_first[None] * even_b[:, None],
            even_real[None] * odd_second[:, None],
            even_imag[None] * odd_second[:, None],
        ],
        axis=1,
    )
    symbol = jnp.dot(
        factors.reshape(8 * HALF, -1), cell_factor, precision=HIGHEST_PRECISION
    ).reshape(2, 4, HALF, rows * NY)
    damp = DAMPING / (HALF * HALF) * jnp.stack(
        [slots * slots, slots_b * slots_b], axis=1
    ).reshape(4).astype(F32)
    return symbol, damp


def off_chip(value):
    return pltpu.with_memory_space_constraint(value, pltpu.HBM)


def stage_forward(density, table):
    planes, points, cells = density.shape
    sent = call(
        forward_kernel,
        [((points * planes, cells), F32)],
        (off_chip(density), off_chip(table["forward_second"])),
        (
            pltpu.VMEM(density.shape, F32),
            pltpu.VMEM((points, 2 * points), BF16),
            pltpu.SemaphoreType.DMA((FORWARD_STEPS + 1,)),
        ),
        flops=6 * points * points * planes * cells,
        keep=False,
        in_specs=[pl.BlockSpec(memory_space=pl.ANY)] * 2,
    )
    return sent.reshape(points // 4, 4, planes, cells)


def stage_local(density, table):
    planes, points, cells = density.shape
    friction, shift = table["friction"], table["column_shift"]
    return call(
        local_kernel,
        [((planes, points, cells), F32)],
        (off_chip(density), off_chip(friction), off_chip(shift)),
        flops=6 * points * points * planes * cells,
        grid=(LOCAL_STEPS,),
        in_specs=[
            pl.BlockSpec((planes // LOCAL_STEPS, points, cells), lambda i: (i, 0, 0)),
            pl.BlockSpec(friction.shape, lambda i: (0, 0)),
            pl.BlockSpec(shift.shape, lambda i: (0, 0, 0)),
        ],
    )


def stage_halo(odd, columns):
    cells = columns.shape[3]
    return call(
        halo_kernel, [((POINTS + POINTS // 4, cells), F32)] * 2, (odd, columns), smem=1
    )


def stage_middle(damp, columns, symbol, table):
    _, _, _, cells = columns.shape
    width = 8 * cells
    scratch = pltpu.VMEM((2 * POINTS, width), BF16)
    return call(
        middle_kernel,
        [(columns.shape, F32)],
        (
            damp,
            columns,
            table["forward_first"],
            symbol,
            table["inverse_first"],
            table["row_inner"],
        ),
        (scratch, scratch),
        20 * POINTS * POINTS * width,
        smem=1,
    )


def stage_edge(odd, partial, halo, odd_band, back=None):
    members, _, planes, cells = partial.shape

    def place(_, odd_ref):
        return (jnp.where(odd_ref[0] == 1, odd_band, 1 - odd_band), 0, 0, 0)

    given = [] if back is None else [off_chip(back)]
    return pl.pallas_call(
        functools.partial(edge_kernel, odd_band),
        out_shape=pltpu.HBM(partial.shape, F32),
        grid_spec=pltpu.PrefetchScalarGridSpec(
            num_scalar_prefetch=1,
            grid=(1,),
            in_specs=[VMEM_SPEC] * 2 + [pl.BlockSpec(memory_space=pl.ANY)] * len(given),
            out_specs=pl.BlockSpec((members // 2, 4, planes, cells), place),
        ),
        input_output_aliases={3: 0} if given else {},
        cost_estimate=pl.CostEstimate(
            flops=20 * partial.size, bytes_accessed=4 * partial.size, transcendentals=0
        ),
        compiler_params=pltpu.CompilerParams(vmem_limit_bytes=24 << 20),
        name="edge_second" if given else "edge_first",
    )(odd, on_chip(partial), on_chip(halo), *given)


def stage_backward(panels, here, table):
    planes, points, cells = here.shape
    return call(
        backward_kernel,
        [((planes, points, cells), F32)],
        (
            on_chip(panels.reshape(points * planes, cells)),
            on_chip(here),
            on_chip(table["inverse_second"]),
        ),
        flops=6 * points * points * planes * cells,
        keep=False,
        grid=(BACKWARD_STEPS,),
        in_specs=[VMEM_SPEC] * 3,
        out_specs=[
            pl.BlockSpec((planes // BACKWARD_STEPS, points, cells), lambda i: (i, 0, 0))
        ],
    )


def local(density, mode_waves, mode_amplitudes, mode_phases):
    _, _, cells = density.shape
    rows_dev = cells // NY
    group = ("pair", "mom")
    strips = lax.axis_size("y")
    table = tables(rows_dev)

    sent = stage_forward(density, table)
    columns = lax.all_to_all(sent, group, split_axis=0, concat_axis=0, tiled=True)
    here = stage_local(density, table)
    position = lax.axis_index("pair") * lax.axis_size("mom") + lax.axis_index("mom")
    odd = (lax.axis_index("y") % 2).reshape(1)
    symbol, damp = symbol_table(
        mode_waves,
        mode_amplitudes,
        mode_phases,
        2 * position,
        lax.axis_index("y") * (2 * rows_dev),
        2 * rows_dev,
        2 * rows_dev * strips,
    )
    first, second = stage_halo(odd, columns)
    links = [(i, (i + 1) % strips) for i in range(strips)]
    swaps = [[p for l in links[start::2] for p in (l, l[::-1])] for start in range(2)]
    first = lax.ppermute(first, "y", swaps[0])
    second = lax.ppermute(second, "y", swaps[1])
    partial = stage_middle(damp, columns, symbol, table)
    back = stage_edge(odd, partial, first, 0)
    back = stage_edge(odd, partial, second, 1, back)
    panels = lax.all_to_all(back, group, split_axis=0, concat_axis=0, tiled=True)
    return stage_backward(panels, here, table)


def solution(mesh):
    bands = mesh.shape["space"]
    finer = jax.sharding.Mesh(
        mesh.devices.reshape(bands // 2, 2, mesh.shape["mom"]), ("y", "pair", "mom")
    )
    return jax.shard_map(
        local,
        mesh=finer,
        in_specs=(P("mom", None, ("y", "pair")), P(), P(), P()),
        out_specs=P("mom", None, ("y", "pair")),
        check_vma=False,
    )
```

```python
import functools
import math

import jax
import jax.numpy as jnp
import ml_dtypes
import numpy as np
from jax import lax
from jax.experimental import pallas as pl
from jax.experimental.pallas import tpu as pltpu
from jax.sharding import PartitionSpec as P

NY = 16
POINTS = 256
HALF = POINTS // 2
DAMPING = 0.5
FRICTION = 0.5
MINUS = ((-3, -2.0), (-2, 15.0), (-1, -60.0), (0, 20.0), (1, 30.0), (2, -3.0))
PLUS = ((3, 2.0), (2, -15.0), (1, 60.0), (0, -20.0), (-1, -30.0), (-2, 3.0))
F32 = jnp.float32
BF16 = jnp.bfloat16
HIGHEST_PRECISION = lax.Precision.HIGHEST
FORWARD_STEPS = 1
BACKWARD_STEPS = 1
LOCAL_STEPS = 2


def wide(table):
    high = table.astype(ml_dtypes.bfloat16)
    low = (table - high.astype(np.float64)).astype(ml_dtypes.bfloat16)
    return np.concatenate([high, low], axis=1)


def real_fourier():
    k = np.arange(POINTS)
    m = np.arange(HALF)
    angles = 2.0 * np.pi / POINTS * (m[:, None] * k[None, :] % POINTS)
    cosine, sine = np.cos(angles), -np.sin(angles)
    sine[0] = 1.0 - 2.0 * (k % 2)
    forward = np.concatenate([cosine, sine], axis=0)
    weight = np.full((HALF,), 2.0)
    weight[0] = 1.0
    inverse = (forward * np.concatenate([weight, weight])[:, None] / POINTS).T
    return forward, inverse


def interleaved(rows):
    return np.stack([rows[:HALF], rows[HALF:]], axis=1).reshape(POINTS, -1)


def friction_matrix():
    speed = (2.0 * np.arange(POINTS) - POINTS + 1) / POINTS
    result = np.zeros((POINTS, POINTS))
    k = np.arange(POINTS - 1)
    result[k, k + 1] = FRICTION * speed[k + 1]
    result[k + 1, k] = -FRICTION * speed[k]
    return result


def row_matrix(stencil, rows):
    result = np.zeros((rows * NY, rows * NY))
    for out_row in range(rows):
        for offset, weight in stencil:
            row = out_row + offset
            if 0 <= row < rows:
                for column in range(NY):
                    result[row * NY + column, out_row * NY + column] = weight
    return result


def column_matrix(stencil, rows):
    result = np.zeros((rows * NY, rows * NY))
    for row in range(rows):
        for column in range(NY):
            for offset, weight in stencil:
                result[row * NY + (column + offset) % NY, row * NY + column] += weight
    return result


def bf16_table(table):
    return jnp.asarray(table.astype(ml_dtypes.bfloat16))


def tables(rows_dev):
    forward, inverse = real_fourier()
    result = {}
    result["forward_second"] = jnp.asarray(wide(interleaved(forward)))
    result["inverse_second"] = jnp.asarray(wide(interleaved(inverse.T).T))
    result["forward_first"] = jnp.asarray(wide(forward))
    friction = friction_matrix().astype(ml_dtypes.bfloat16)
    result["inverse_first"] = jnp.asarray(wide(inverse))
    result["friction"] = jnp.asarray(np.concatenate([friction, friction], axis=1))
    rows = 2 * rows_dev
    result["row_inner"] = bf16_table(
        np.stack([row_matrix(stencil, rows) for stencil in (PLUS, MINUS)])
    )
    result["column_shift"] = bf16_table(
        np.stack(
            [
                np.concatenate([column_matrix(s, rows_dev)] * 2, axis=0)
                for s in (PLUS, MINUS)
            ]
        )
    )
    return result


def split(value):
    high = value.astype(BF16)
    low = (value - high.astype(F32)).astype(BF16)
    return high, low


def dot(left, right):
    return jnp.dot(left, right, preferred_element_type=F32)


def wide_dot(table, high, low):
    first, second = table[:, :POINTS], table[:, POINTS : 2 * POINTS]
    return dot(
        jnp.concatenate([first, first, second], axis=1),
        jnp.concatenate([high, low, high], axis=0),
    )


def speed_over_60(first, count, width):
    index = first + lax.broadcasted_iota(jnp.int32, (count, width), 0)
    return (2 * index - (POINTS - 1)).astype(F32) * (1.0 / (60 * POINTS))


def forward_kernel(u_hbm, table_hbm, out_ref, u_ref, table_ref, sems):
    planes, _, cells = u_ref.shape
    step = planes // FORWARD_STEPS
    table_copy = pltpu.make_async_copy(table_hbm, table_ref, sems.at[FORWARD_STEPS])
    copies = [
        pltpu.make_async_copy(
            u_hbm.at[pl.ds(i * step, step)], u_ref.at[pl.ds(i * step, step)], sems.at[i]
        )
        for i in range(FORWARD_STEPS)
    ]
    copies[0].start()
    table_copy.start()
    for copy in copies[1:]:
        copy.start()
    for i, copy in enumerate(copies):
        copy.wait()
        if i == 0:
            table_copy.wait()
        parts = [split(u_ref[k]) for k in range(i * step, (i + 1) * step)]
        high, low = (jnp.concatenate(values, axis=1) for values in zip(*parts))
        result = wide_dot(table_ref[...], high, low)
        for k in range(step):
            out_ref[pl.ds(i * step + k, POINTS, stride=planes), :] = result[
                :, k * cells : (k + 1) * cells
            ]


def backward_kernel(w_ref, local_ref, table_ref, out_ref):
    planes, _, cells = out_ref.shape
    first = pl.program_id(0) * planes
    stride = w_ref.shape[0] // POINTS
    parts = [
        split(w_ref[pl.ds(first + k, POINTS, stride=stride), :]) for k in range(planes)
    ]
    high, low = (jnp.concatenate(values, axis=1) for values in zip(*parts))
    result = wide_dot(table_ref[...], high, low)
    for k in range(planes):
        out_ref[k] = result[:, k * cells : (k + 1) * cells] + local_ref[first + k]


def local_kernel(u_ref, friction_ref, shift_ref, out_ref):
    planes, _, cells = u_ref.shape
    first = pl.program_id(0) * planes
    for k in range(planes):
        high, low = split(u_ref[k])
        friction = dot(friction_ref[...], jnp.concatenate([high, low], axis=0))
        both = jnp.concatenate([high, low], axis=1)
        for side in range(2):
            part = slice(side * HALF, (side + 1) * HALF)
            moved = dot(both[part], shift_ref[side])
            out_ref[first + k, part, :] = friction[part] - moved * speed_over_60(
                side * HALF, HALF, cells
            )


def lane_select(values, lane, width):
    result = values[0]
    for index, value in enumerate(values[1:], 1):
        result = jnp.where(lane >= index * width, value, result)
    return result


def turn(value, shift):
    shift %= value.shape[1]
    return pltpu.roll(value, shift, 1) if shift else value


def pack(r_ref, near, far, side):
    cells = r_ref.shape[3]
    lane = lax.broadcasted_iota(jnp.int32, (POINTS, cells), 1)
    columns = [r_ref[:, q].reshape(POINTS, cells) for q in range(4)]
    wide_part = lane_select(
        [turn(v, 2 * NY * q - near) for q, v in enumerate(columns)], lane, 2 * NY
    )
    quarter = HALF // 2
    lane = lane[:quarter]
    thin_part = lane_select(
        [
            turn(columns[q][side * HALF + h * quarter : side * HALF + (h + 1) * quarter], NY * (q + 4 * h) - far)
            for h in range(2)
            for q in range(4)
        ],
        lane,
        NY,
    )
    return wide_part, thin_part


def halo_kernel(odd_ref, r_ref, first_ref, second_ref):
    owners = r_ref.shape[0] // 2
    cells = r_ref.shape[3]
    odd = odd_ref[0] == 1
    up = pack(r_ref.at[owners:], cells - 2 * NY, cells - 3 * NY, 1)
    down = pack(r_ref.at[:owners], 0, 2 * NY, 0)
    at = 0
    for upper, lower in zip(up, down):
        rows = upper.shape[0]
        first_ref[at : at + rows, :] = jnp.where(odd, lower, upper)
        second_ref[at : at + rows, :] = jnp.where(odd, upper, lower)
        at += rows


def load_columns(r_ref, x_ref):
    owners = r_ref.shape[0] // 2
    cells = r_ref.shape[3]
    for q in range(4):
        for side in range(2):
            value = r_ref[side * owners : (side + 1) * owners, q].reshape(POINTS, cells)
            high, low = split(value)
            at = (2 * q + side) * cells
            x_ref[0:POINTS, at : at + cells] = high
            x_ref[POINTS : 2 * POINTS, at : at + cells] = low


def first_friction(value):
    index = lax.broadcasted_iota(jnp.int32, value.shape, 0)
    weighted = value * (
        (2 * index - (POINTS - 1)).astype(F32) * (FRICTION / POINTS)
    )
    later = jnp.where(index < POINTS - 1, pltpu.roll(weighted, POINTS - 1, 0), 0.0)
    earlier = jnp.where(index > 0, pltpu.roll(weighted, 1, 0), 0.0)
    return later - earlier


def middle_kernel(
    damp_ref, r_ref, forward_ref, symbol_ref, inverse_ref, inner_ref, out_ref, x_ref, y_ref
):
    load_columns(r_ref, x_ref)
    spectrum = wide_dot(forward_ref[...], x_ref[0:POINTS, :], x_ref[POINTS:, :])
    width = spectrum.shape[1] // 4
    row = lax.broadcasted_iota(jnp.int32, (HALF, width), 0)
    scale = DAMPING / (HALF * HALF)
    damp_real = scale * (row * row).astype(F32)
    row_imag = jnp.where(row == 0, HALF, row)
    damp_imag = scale * (row_imag * row_imag).astype(F32)
    for slot in range(2):
        qa, qb = 2 * slot, 2 * slot + 1
        real_a, imag_a = (
            spectrum[h * HALF : (h + 1) * HALF, qa * width : (qa + 1) * width]
            for h in range(2)
        )
        real_b, imag_b = (
            spectrum[h * HALF : (h + 1) * HALF, qb * width : (qb + 1) * width]
            for h in range(2)
        )
        odd_a, odd_b = symbol_ref[slot, 0], symbol_ref[slot, 1]
        even_real, even_imag = symbol_ref[slot, 2], symbol_ref[slot, 3]
        da, db = damp_ref[qa], damp_ref[qb]
        results = (
            (qa, 0, -odd_a * imag_a - even_real * real_b - (damp_real + da) * real_a),
            (qa, 1, odd_a * real_a - even_imag * imag_b - (damp_imag + da) * imag_a),
            (qb, 0, -odd_b * imag_b + even_real * real_a - (damp_real + db) * real_b),
            (qb, 1, odd_b * real_b + even_imag * imag_a - (damp_imag + db) * imag_b),
        )
        for q, half, value in results:
            high, low = split(value)
            at = q * width
            y_ref[half * HALF : (half + 1) * HALF, at : at + width] = high
            y_ref[POINTS + half * HALF : POINTS + (half + 1) * HALF, at : at + width] = low
    cells = width // 2
    owners = out_ref.shape[0] // 2
    result = wide_dot(inverse_ref[...], y_ref[0:POINTS, :], y_ref[POINTS:, :])
    moved = [
        dot(
            jnp.concatenate(
                [
                    jnp.concatenate(
                        [
                            x_ref[
                                half + side * HALF : half + (side + 1) * HALF,
                                q * width : (q + 1) * width,
                            ]
                            for half in (0, POINTS)
                        ],
                        axis=1,
                    )
                    for q in range(4)
                ],
                axis=0,
            ),
            jnp.concatenate([inner_ref[side]] * 2, axis=0),
        )
        for side in range(2)
    ]
    rows = owners // 2
    for q in range(4):
        for band in range(2):
            here = r_ref[band * owners : (band + 1) * owners, q].reshape(POINTS, cells)
            friction = first_friction(here)
            inside = slice(band * cells, (band + 1) * cells)
            for side in range(2):
                part = slice(side * HALF, (side + 1) * HALF)
                value = (
                    result[part, q * width : (q + 1) * width][:, inside]
                    + friction[part]
                    - moved[side][q * HALF : (q + 1) * HALF, inside]
                    * speed_over_60(side * HALF, HALF, cells)
                )
                at = band * owners + side * rows
                out_ref[at : at + rows, q] = value.reshape(rows, -1, cells)


def lane_weight(lane, first_row, last_row, weight):
    return jnp.where((lane >= first_row * NY) & (lane < last_row * NY), weight, 0.0)


def edge_kernel(odd_band, odd_ref, partial_ref, halo_ref, *refs):
    out_ref = refs[-1]
    for odd in range(2):

        @pl.when(odd_ref[0] == odd)
        def _(band=odd_band if odd else 1 - odd_band):
            for side in range(2):
                edge_part(band, side, partial_ref, halo_ref, out_ref)


def edge_part(band, side, partial_ref, halo_ref, out_ref):
    members, _, _, cells = out_ref.shape
    owners = members // 2
    band_rows = cells // NY
    stencil = dict((PLUS, MINUS)[side])
    weights = [stencil.get(s if band else -s) for s in (1, 2, 3)]
    lane = lax.broadcasted_iota(jnp.int32, (HALF, cells), 1)
    pair = halo_ref[side * HALF : (side + 1) * HALF, :]
    thin = halo_ref[POINTS : POINTS + HALF // 2, :]
    speed = speed_over_60(side * HALF, HALF, cells)
    here = slice(side * owners, (side + 1) * owners)
    block = slice((2 * band + side) * owners, (2 * band + side + 1) * owners)
    for q in range(4):
        moved = 0.0
        for s, weight in enumerate(weights, 1):
            if weight is None:
                continue
            if band:
                near = band_rows - s
                rows = (near, min(near + 2, band_rows))
            else:
                near = s - 2
                rows = (max(near, 0), s)
            moved += lane_weight(lane, *rows, weight) * turn(pair, NY * (near - 2 * q))
        if weights[2] is not None:
            row = band_rows - 1 if band else 0
            third = jnp.concatenate(
                [turn(thin, NY * (row - q - 4 * h)) for h in range(2)], axis=0
            )
            moved += lane_weight(lane, row, row + 1, weights[2]) * third
        out_ref[here, q] = partial_ref[block, q] - (moved * speed).reshape(owners, -1, cells)


VMEM_SPEC = pl.BlockSpec(memory_space=pltpu.VMEM)
SMEM_SPEC = pl.BlockSpec(memory_space=pltpu.SMEM)


def on_chip(value):
    return pltpu.with_memory_space_constraint(value, pltpu.VMEM)


def call(
    kernel,
    shapes,
    inputs,
    scratch=(),
    flops=1,
    smem=0,
    keep=True,
    grid=(),
    in_specs=None,
    out_specs=None,
):
    bytes_accessed = sum(v.size * v.dtype.itemsize for v in inputs)
    shapes = [pltpu.VMEM(*s) if keep else jax.ShapeDtypeStruct(*s) for s in shapes]
    if in_specs is None:
        inputs = [*inputs[:smem], *(on_chip(v) for v in inputs[smem:])]
        in_specs = [SMEM_SPEC] * smem + [VMEM_SPEC] * (len(inputs) - smem)
    if out_specs is None:
        out_specs = [VMEM_SPEC] * len(shapes)
    single = len(shapes) == 1
    return pl.pallas_call(
        kernel,
        grid=grid,
        out_shape=shapes[0] if single else shapes,
        in_specs=in_specs,
        out_specs=out_specs[0] if single else out_specs,
        scratch_shapes=list(scratch),
        cost_estimate=pl.CostEstimate(
            flops=flops, bytes_accessed=2 * bytes_accessed, transcendentals=0
        ),
        compiler_params=pltpu.CompilerParams(vmem_limit_bytes=24 << 20),
    )(*inputs)


def symbol_table(mode_waves, mode_amplitudes, mode_phases, first_slot, first_row, rows, total_rows):
    local = jnp.arange(rows * NY, dtype=jnp.int32)
    row, column = first_row + local // NY, local % NY
    turn_rows = mode_waves[:, 0:1] * row[None, :] % total_rows
    turn_columns = mode_waves[:, 1:2] * column[None, :] % NY
    angles = (
        2.0
        * math.pi
        * (turn_rows.astype(F32) / total_rows + turn_columns.astype(F32) / NY)
        + mode_phases[:, None]
    )
    cell_factor = mode_amplitudes[:, None] * jnp.sin(angles)
    scale = math.pi / POINTS

    def turned(waves, frequency):
        return scale * (waves * frequency % (2 * POINTS)).astype(F32)

    first_waves, second_waves = mode_waves[None, :, 0], mode_waves[None, :, 1]
    real_freq = jnp.arange(HALF, dtype=jnp.int32)[:, None]
    imag_freq = jnp.where(real_freq == 0, HALF, real_freq)
    odd_first = jnp.sin(turned(first_waves, real_freq))
    even_real = jnp.cos(turned(first_waves, real_freq))
    even_imag = jnp.cos(turned(first_waves, imag_freq))
    slots = first_slot + jnp.arange(2, dtype=jnp.int32)[:, None]
    slots_b = jnp.where(slots == 0, HALF, slots)
    odd_second = jnp.sin(turned(second_waves, slots))
    even_a = jnp.cos(turned(second_waves, slots))
    even_b = jnp.cos(turned(second_waves, slots_b))
    factors = jnp.stack(
        [
            odd_first[None] * even_a[:, None],
            odd_first[None] * even_b[:, None],
            even_real[None] * odd_second[:, None],
            even_imag[None] * odd_second[:, None],
        ],
        axis=1,
    )
    symbol = jnp.dot(
        factors.reshape(8 * HALF, -1), cell_factor, precision=HIGHEST_PRECISION
    ).reshape(2, 4, HALF, rows * NY)
    damp = DAMPING / (HALF * HALF) * jnp.stack(
        [slots * slots, slots_b * slots_b], axis=1
    ).reshape(4).astype(F32)
    return symbol, damp


def off_chip(value):
    return pltpu.with_memory_space_constraint(value, pltpu.HBM)


def stage_forward(density, table):
    planes, points, cells = density.shape
    sent = call(
        forward_kernel,
        [((points * planes, cells), F32)],
        (off_chip(density), off_chip(table["forward_second"])),
        (
            pltpu.VMEM(density.shape, F32),
            pltpu.VMEM((points, 2 * points), BF16),
            pltpu.SemaphoreType.DMA((FORWARD_STEPS + 1,)),
        ),
        flops=6 * points * points * planes * cells,
        keep=False,
        in_specs=[pl.BlockSpec(memory_space=pl.ANY)] * 2,
    )
    return sent.reshape(points // 4, 4, planes, cells)


def stage_local(density, table):
    planes, points, cells = density.shape
    friction, shift = table["friction"], table["column_shift"]
    return call(
        local_kernel,
        [((planes, points, cells), F32)],
        (off_chip(density), off_chip(friction), off_chip(shift)),
        flops=6 * points * points * planes * cells,
        grid=(LOCAL_STEPS,),
        in_specs=[
            pl.BlockSpec((planes // LOCAL_STEPS, points, cells), lambda i: (i, 0, 0)),
            pl.BlockSpec(friction.shape, lambda i: (0, 0)),
            pl.BlockSpec(shift.shape, lambda i: (0, 0, 0)),
        ],
    )


def stage_halo(odd, columns):
    cells = columns.shape[3]
    return call(
        halo_kernel, [((POINTS + POINTS // 4, cells), F32)] * 2, (odd, columns), smem=1
    )


def stage_middle(damp, columns, symbol, table):
    _, _, _, cells = columns.shape
    width = 8 * cells
    scratch = pltpu.VMEM((2 * POINTS, width), BF16)
    return call(
        middle_kernel,
        [(columns.shape, F32)],
        (
            damp,
            columns,
            table["forward_first"],
            symbol,
            table["inverse_first"],
            table["row_inner"],
        ),
        (scratch, scratch),
        20 * POINTS * POINTS * width,
        smem=1,
    )


def stage_edge(odd, partial, halo, odd_band, back=None):
    members, _, planes, cells = partial.shape

    def place(_, odd_ref):
        return (jnp.where(odd_ref[0] == 1, odd_band, 1 - odd_band), 0, 0, 0)

    given = [] if back is None else [off_chip(back)]
    return pl.pallas_call(
        functools.partial(edge_kernel, odd_band),
        out_shape=pltpu.HBM(partial.shape, F32),
        grid_spec=pltpu.PrefetchScalarGridSpec(
            num_scalar_prefetch=1,
            grid=(1,),
            in_specs=[VMEM_SPEC] * 2 + [pl.BlockSpec(memory_space=pl.ANY)] * len(given),
            out_specs=pl.BlockSpec((members // 2, 4, planes, cells), place),
        ),
        input_output_aliases={3: 0} if given else {},
        cost_estimate=pl.CostEstimate(
            flops=20 * partial.size, bytes_accessed=4 * partial.size, transcendentals=0
        ),
        compiler_params=pltpu.CompilerParams(vmem_limit_bytes=24 << 20),
        name="edge_second" if given else "edge_first",
    )(odd, on_chip(partial), on_chip(halo), *given)


def stage_backward(panels, here, table):
    planes, points, cells = here.shape
    return call(
        backward_kernel,
        [((planes, points, cells), F32)],
        (
            on_chip(panels.reshape(points * planes, cells)),
            on_chip(here),
            on_chip(table["inverse_second"]),
        ),
        flops=6 * points * points * planes * cells,
        keep=False,
        grid=(BACKWARD_STEPS,),
        in_specs=[VMEM_SPEC] * 3,
        out_specs=[
            pl.BlockSpec((planes // BACKWARD_STEPS, points, cells), lambda i: (i, 0, 0))
        ],
    )


def local(density, mode_waves, mode_amplitudes, mode_phases):
    _, _, cells = density.shape
    rows_dev = cells // NY
    group = ("pair", "mom")
    strips = lax.axis_size("y")
    table = tables(rows_dev)

    sent = stage_forward(density, table)
    columns = lax.all_to_all(sent, group, split_axis=0, concat_axis=0, tiled=True)
    here = stage_local(density, table)
    position = lax.axis_index("pair") * lax.axis_size("mom") + lax.axis_index("mom")
    odd = (lax.axis_index("y") % 2).reshape(1)
    symbol, damp = symbol_table(
        mode_waves,
        mode_amplitudes,
        mode_phases,
        2 * position,
        lax.axis_index("y") * (2 * rows_dev),
        2 * rows_dev,
        2 * rows_dev * strips,
    )
    first, second = stage_halo(odd, columns)
    links = [(i, (i + 1) % strips) for i in range(strips)]
    swaps = [[p for l in links[start::2] for p in (l, l[::-1])] for start in range(2)]
    first = lax.ppermute(first, "y", swaps[0])
    second = lax.ppermute(second, "y", swaps[1])
    partial = stage_middle(damp, columns, symbol, table)
    back = stage_edge(odd, partial, first, 0)
    back = stage_edge(odd, partial, second, 1, back)
    panels = lax.all_to_all(back, group, split_axis=0, concat_axis=0, tiled=True)
    return stage_backward(panels, here, table)


def solution(mesh):
    bands = mesh.shape["space"]
    finer = jax.sharding.Mesh(
        mesh.devices.reshape(bands // 2, 2, mesh.shape["mom"]), ("y", "pair", "mom")
    )
    return jax.shard_map(
        local,
        mesh=finer,
        in_specs=(P("mom", None, ("y", "pair")), P(), P(), P()),
        out_specs=P("mom", None, ("y", "pair")),
        check_vma=False,
    )
```

```python
import functools
import math

import jax
import jax.numpy as jnp
import ml_dtypes
import numpy as np
from jax import lax
from jax.experimental import pallas as pl
from jax.experimental.pallas import tpu as pltpu
from jax.sharding import PartitionSpec as P

NY = 16
POINTS = 256
HALF = POINTS // 2
DAMPING = 0.5
FRICTION = 0.5
MINUS = ((-3, -2.0), (-2, 15.0), (-1, -60.0), (0, 20.0), (1, 30.0), (2, -3.0))
PLUS = ((3, 2.0), (2, -15.0), (1, 60.0), (0, -20.0), (-1, -30.0), (-2, 3.0))
F32 = jnp.float32
BF16 = jnp.bfloat16
HIGHEST_PRECISION = lax.Precision.HIGHEST
FORWARD_STEPS = 1
BACKWARD_STEPS = 1
LOCAL_STEPS = 2


def wide(table):
    high = table.astype(ml_dtypes.bfloat16)
    low = (table - high.astype(np.float64)).astype(ml_dtypes.bfloat16)
    return np.concatenate([high, low], axis=1)


def real_fourier():
    k = np.arange(POINTS)
    m = np.arange(HALF)
    angles = 2.0 * np.pi / POINTS * (m[:, None] * k[None, :] % POINTS)
    cosine, sine = np.cos(angles), -np.sin(angles)
    sine[0] = 1.0 - 2.0 * (k % 2)
    forward = np.concatenate([cosine, sine], axis=0)
    weight = np.full((HALF,), 2.0)
    weight[0] = 1.0
    inverse = (forward * np.concatenate([weight, weight])[:, None] / POINTS).T
    return forward, inverse


def interleaved(rows):
    return np.stack([rows[:HALF], rows[HALF:]], axis=1).reshape(POINTS, -1)


def friction_matrix():
    speed = (2.0 * np.arange(POINTS) - POINTS + 1) / POINTS
    result = np.zeros((POINTS, POINTS))
    k = np.arange(POINTS - 1)
    result[k, k + 1] = FRICTION * speed[k + 1]
    result[k + 1, k] = -FRICTION * speed[k]
    return result


def row_matrix(stencil, rows):
    result = np.zeros((rows * NY, rows * NY))
    for out_row in range(rows):
        for offset, weight in stencil:
            row = out_row + offset
            if 0 <= row < rows:
                for column in range(NY):
                    result[row * NY + column, out_row * NY + column] = weight
    return result


def column_matrix(stencil, rows):
    result = np.zeros((rows * NY, rows * NY))
    for row in range(rows):
        for column in range(NY):
            for offset, weight in stencil:
                result[row * NY + (column + offset) % NY, row * NY + column] += weight
    return result


def bf16_table(table):
    return jnp.asarray(table.astype(ml_dtypes.bfloat16))


def tables(rows_dev):
    forward, inverse = real_fourier()
    result = {}
    result["forward_second"] = jnp.asarray(wide(interleaved(forward)))
    result["inverse_second"] = jnp.asarray(wide(interleaved(inverse.T).T))
    result["forward_first"] = jnp.asarray(wide(forward))
    friction = friction_matrix().astype(ml_dtypes.bfloat16)
    result["inverse_first"] = jnp.asarray(wide(inverse))
    result["friction"] = jnp.asarray(np.concatenate([friction, friction], axis=1))
    rows = 2 * rows_dev
    result["row_inner"] = bf16_table(
        np.stack([row_matrix(stencil, rows) for stencil in (PLUS, MINUS)])
    )
    result["column_shift"] = bf16_table(
        np.stack(
            [
                np.concatenate([column_matrix(s, rows_dev)] * 2, axis=0)
                for s in (PLUS, MINUS)
            ]
        )
    )
    return result


def split(value):
    high = value.astype(BF16)
    low = (value - high.astype(F32)).astype(BF16)
    return high, low


def dot(left, right):
    return jnp.dot(left, right, preferred_element_type=F32)


def wide_dot(table, high, low):
    first, second = table[:, :POINTS], table[:, POINTS : 2 * POINTS]
    return dot(
        jnp.concatenate([first, first, second], axis=1),
        jnp.concatenate([high, low, high], axis=0),
    )


def speed_over_60(first, count, width):
    index = first + lax.broadcasted_iota(jnp.int32, (count, width), 0)
    return (2 * index - (POINTS - 1)).astype(F32) * (1.0 / (60 * POINTS))


def forward_kernel(u_hbm, table_hbm, out_ref, u_ref, table_ref, sems):
    planes, _, cells = u_ref.shape
    step = planes // FORWARD_STEPS
    table_copy = pltpu.make_async_copy(table_hbm, table_ref, sems.at[FORWARD_STEPS])
    copies = [
        pltpu.make_async_copy(
            u_hbm.at[pl.ds(i * step, step)], u_ref.at[pl.ds(i * step, step)], sems.at[i]
        )
        for i in range(FORWARD_STEPS)
    ]
    copies[0].start()
    table_copy.start()
    for copy in copies[1:]:
        copy.start()
    for i, copy in enumerate(copies):
        copy.wait()
        if i == 0:
            table_copy.wait()
        parts = [split(u_ref[k]) for k in range(i * step, (i + 1) * step)]
        high, low = (jnp.concatenate(values, axis=1) for values in zip(*parts))
        result = wide_dot(table_ref[...], high, low)
        for k in range(step):
            out_ref[pl.ds(i * step + k, POINTS, stride=planes), :] = result[
                :, k * cells : (k + 1) * cells
            ]


def backward_kernel(w_ref, local_ref, table_ref, out_ref):
    planes, _, cells = out_ref.shape
    first = pl.program_id(0) * planes
    stride = w_ref.shape[0] // POINTS
    parts = [
        split(w_ref[pl.ds(first + k, POINTS, stride=stride), :]) for k in range(planes)
    ]
    high, low = (jnp.concatenate(values, axis=1) for values in zip(*parts))
    result = wide_dot(table_ref[...], high, low)
    for k in range(planes):
        out_ref[k] = result[:, k * cells : (k + 1) * cells] + local_ref[first + k]


def local_kernel(u_ref, friction_ref, shift_ref, out_ref):
    planes, _, cells = u_ref.shape
    first = pl.program_id(0) * planes
    for k in range(planes):
        high, low = split(u_ref[k])
        friction = dot(friction_ref[...], jnp.concatenate([high, low], axis=0))
        both = jnp.concatenate([high, low], axis=1)
        for side in range(2):
            part = slice(side * HALF, (side + 1) * HALF)
            moved = dot(both[part], shift_ref[side])
            out_ref[first + k, part, :] = friction[part] - moved * speed_over_60(
                side * HALF, HALF, cells
            )


def lane_select(values, lane, width):
    result = values[0]
    for index, value in enumerate(values[1:], 1):
        result = jnp.where(lane >= index * width, value, result)
    return result


def turn(value, shift):
    shift %= value.shape[1]
    return pltpu.roll(value, shift, 1) if shift else value


def pack(r_ref, near, far, side):
    cells = r_ref.shape[3]
    lane = lax.broadcasted_iota(jnp.int32, (POINTS, cells), 1)
    columns = [r_ref[:, q].reshape(POINTS, cells) for q in range(4)]
    wide_part = lane_select(
        [turn(v, 2 * NY * q - near) for q, v in enumerate(columns)], lane, 2 * NY
    )
    quarter = HALF // 2
    lane = lane[:quarter]
    thin_part = lane_select(
        [
            turn(columns[q][side * HALF + h * quarter : side * HALF + (h + 1) * quarter], NY * (q + 4 * h) - far)
            for h in range(2)
            for q in range(4)
        ],
        lane,
        NY,
    )
    return wide_part, thin_part


def halo_kernel(odd_ref, r_ref, first_ref, second_ref):
    owners = r_ref.shape[0] // 2
    cells = r_ref.shape[3]
    odd = odd_ref[0] == 1
    up = pack(r_ref.at[owners:], cells - 2 * NY, cells - 3 * NY, 1)
    down = pack(r_ref.at[:owners], 0, 2 * NY, 0)
    at = 0
    for upper, lower in zip(up, down):
        rows = upper.shape[0]
        first_ref[at : at + rows, :] = jnp.where(odd, lower, upper)
        second_ref[at : at + rows, :] = jnp.where(odd, upper, lower)
        at += rows


def load_columns(r_ref, x_ref):
    owners = r_ref.shape[0] // 2
    cells = r_ref.shape[3]
    for q in range(4):
        for side in range(2):
            value = r_ref[side * owners : (side + 1) * owners, q].reshape(POINTS, cells)
            high, low = split(value)
            at = (2 * q + side) * cells
            x_ref[0:POINTS, at : at + cells] = high
            x_ref[POINTS : 2 * POINTS, at : at + cells] = low


def first_friction(value):
    index = lax.broadcasted_iota(jnp.int32, value.shape, 0)
    weighted = value * (
        (2 * index - (POINTS - 1)).astype(F32) * (FRICTION / POINTS)
    )
    later = jnp.where(index < POINTS - 1, pltpu.roll(weighted, POINTS - 1, 0), 0.0)
    earlier = jnp.where(index > 0, pltpu.roll(weighted, 1, 0), 0.0)
    return later - earlier


def middle_kernel(
    damp_ref, r_ref, forward_ref, symbol_ref, inverse_ref, inner_ref, out_ref, x_ref, y_ref
):
    load_columns(r_ref, x_ref)
    spectrum = wide_dot(forward_ref[...], x_ref[0:POINTS, :], x_ref[POINTS:, :])
    width = spectrum.shape[1] // 4
    row = lax.broadcasted_iota(jnp.int32, (HALF, width), 0)
    scale = DAMPING / (HALF * HALF)
    damp_real = scale * (row * row).astype(F32)
    row_imag = jnp.where(row == 0, HALF, row)
    damp_imag = scale * (row_imag * row_imag).astype(F32)
    for slot in range(2):
        qa, qb = 2 * slot, 2 * slot + 1
        real_a, imag_a = (
            spectrum[h * HALF : (h + 1) * HALF, qa * width : (qa + 1) * width]
            for h in range(2)
        )
        real_b, imag_b = (
            spectrum[h * HALF : (h + 1) * HALF, qb * width : (qb + 1) * width]
            for h in range(2)
        )
        odd_a, odd_b = symbol_ref[slot, 0], symbol_ref[slot, 1]
        even_real, even_imag = symbol_ref[slot, 2], symbol_ref[slot, 3]
        da, db = damp_ref[qa], damp_ref[qb]
        results = (
            (qa, 0, -odd_a * imag_a - even_real * real_b - (damp_real + da) * real_a),
            (qa, 1, odd_a * real_a - even_imag * imag_b - (damp_imag + da) * imag_a),
            (qb, 0, -odd_b * imag_b + even_real * real_a - (damp_real + db) * real_b),
            (qb, 1, odd_b * real_b + even_imag * imag_a - (damp_imag + db) * imag_b),
        )
        for q, half, value in results:
            high, low = split(value)
            at = q * width
            y_ref[half * HALF : (half + 1) * HALF, at : at + width] = high
            y_ref[POINTS + half * HALF : POINTS + (half + 1) * HALF, at : at + width] = low
    cells = width // 2
    owners = out_ref.shape[0] // 2
    result = wide_dot(inverse_ref[...], y_ref[0:POINTS, :], y_ref[POINTS:, :])
    moved = [
        dot(
            jnp.concatenate(
                [
                    jnp.concatenate(
                        [
                            x_ref[
                                half + side * HALF : half + (side + 1) * HALF,
                                q * width : (q + 1) * width,
                            ]
                            for half in (0, POINTS)
                        ],
                        axis=1,
                    )
                    for q in range(4)
                ],
                axis=0,
            ),
            jnp.concatenate([inner_ref[side]] * 2, axis=0),
        )
        for side in range(2)
    ]
    rows = owners // 2
    for q in range(4):
        for band in range(2):
            here = r_ref[band * owners : (band + 1) * owners, q].reshape(POINTS, cells)
            friction = first_friction(here)
            inside = slice(band * cells, (band + 1) * cells)
            for side in range(2):
                part = slice(side * HALF, (side + 1) * HALF)
                value = (
                    result[part, q * width : (q + 1) * width][:, inside]
                    + friction[part]
                    - moved[side][q * HALF : (q + 1) * HALF, inside]
                    * speed_over_60(side * HALF, HALF, cells)
                )
                at = band * owners + side * rows
                out_ref[at : at + rows, q] = value.reshape(rows, -1, cells)


def lane_weight(lane, first_row, last_row, weight):
    return jnp.where((lane >= first_row * NY) & (lane < last_row * NY), weight, 0.0)


def edge_kernel(odd_band, odd_ref, partial_ref, halo_ref, out_ref):
    for odd in range(2):

        @pl.when(odd_ref[0] == odd)
        def _(band=odd_band if odd else 1 - odd_band):
            for side in range(2):
                edge_part(band, side, partial_ref, halo_ref, out_ref)


def edge_second_kernel(odd_ref, partial_ref, halo_ref, done_ref, out_ref):
    @pl.when(pl.program_id(0) == 0)
    def _():
        out_ref[...] = done_ref[...]

    @pl.when(pl.program_id(0) == 1)
    def _():
        edge_kernel(1, odd_ref, partial_ref, halo_ref, out_ref)


def edge_part(band, side, partial_ref, halo_ref, out_ref):
    members, _, _, cells = out_ref.shape
    owners = members // 2
    band_rows = cells // NY
    stencil = dict((PLUS, MINUS)[side])
    weights = [stencil.get(s if band else -s) for s in (1, 2, 3)]
    lane = lax.broadcasted_iota(jnp.int32, (HALF, cells), 1)
    pair = halo_ref[side * HALF : (side + 1) * HALF, :]
    thin = halo_ref[POINTS : POINTS + HALF // 2, :]
    speed = speed_over_60(side * HALF, HALF, cells)
    here = slice(side * owners, (side + 1) * owners)
    block = slice((2 * band + side) * owners, (2 * band + side + 1) * owners)
    for q in range(4):
        moved = 0.0
        for s, weight in enumerate(weights, 1):
            if weight is None:
                continue
            if band:
                near = band_rows - s
                rows = (near, min(near + 2, band_rows))
            else:
                near = s - 2
                rows = (max(near, 0), s)
            moved += lane_weight(lane, *rows, weight) * turn(pair, NY * (near - 2 * q))
        if weights[2] is not None:
            row = band_rows - 1 if band else 0
            third = jnp.concatenate(
                [turn(thin, NY * (row - q - 4 * h)) for h in range(2)], axis=0
            )
            moved += lane_weight(lane, row, row + 1, weights[2]) * third
        out_ref[here, q] = partial_ref[block, q] - (moved * speed).reshape(owners, -1, cells)


VMEM_SPEC = pl.BlockSpec(memory_space=pltpu.VMEM)
SMEM_SPEC = pl.BlockSpec(memory_space=pltpu.SMEM)


def on_chip(value):
    return pltpu.with_memory_space_constraint(value, pltpu.VMEM)


def call(
    kernel,
    shapes,
    inputs,
    scratch=(),
    flops=1,
    smem=0,
    keep=True,
    grid=(),
    in_specs=None,
    out_specs=None,
):
    bytes_accessed = sum(v.size * v.dtype.itemsize for v in inputs)
    shapes = [pltpu.VMEM(*s) if keep else jax.ShapeDtypeStruct(*s) for s in shapes]
    if in_specs is None:
        inputs = [*inputs[:smem], *(on_chip(v) for v in inputs[smem:])]
        in_specs = [SMEM_SPEC] * smem + [VMEM_SPEC] * (len(inputs) - smem)
    if out_specs is None:
        out_specs = [VMEM_SPEC] * len(shapes)
    single = len(shapes) == 1
    return pl.pallas_call(
        kernel,
        grid=grid,
        out_shape=shapes[0] if single else shapes,
        in_specs=in_specs,
        out_specs=out_specs[0] if single else out_specs,
        scratch_shapes=list(scratch),
        cost_estimate=pl.CostEstimate(
            flops=flops, bytes_accessed=2 * bytes_accessed, transcendentals=0
        ),
        compiler_params=pltpu.CompilerParams(vmem_limit_bytes=24 << 20),
    )(*inputs)


def symbol_table(mode_waves, mode_amplitudes, mode_phases, first_slot, first_row, rows, total_rows):
    local = jnp.arange(rows * NY, dtype=jnp.int32)
    row, column = first_row + local // NY, local % NY
    turn_rows = mode_waves[:, 0:1] * row[None, :] % total_rows
    turn_columns = mode_waves[:, 1:2] * column[None, :] % NY
    angles = (
        2.0
        * math.pi
        * (turn_rows.astype(F32) / total_rows + turn_columns.astype(F32) / NY)
        + mode_phases[:, None]
    )
    cell_factor = mode_amplitudes[:, None] * jnp.sin(angles)
    scale = math.pi / POINTS

    def turned(waves, frequency):
        return scale * (waves * frequency % (2 * POINTS)).astype(F32)

    first_waves, second_waves = mode_waves[None, :, 0], mode_waves[None, :, 1]
    real_freq = jnp.arange(HALF, dtype=jnp.int32)[:, None]
    imag_freq = jnp.where(real_freq == 0, HALF, real_freq)
    odd_first = jnp.sin(turned(first_waves, real_freq))
    even_real = jnp.cos(turned(first_waves, real_freq))
    even_imag = jnp.cos(turned(first_waves, imag_freq))
    slots = first_slot + jnp.arange(2, dtype=jnp.int32)[:, None]
    slots_b = jnp.where(slots == 0, HALF, slots)
    odd_second = jnp.sin(turned(second_waves, slots))
    even_a = jnp.cos(turned(second_waves, slots))
    even_b = jnp.cos(turned(second_waves, slots_b))
    factors = jnp.stack(
        [
            odd_first[None] * even_a[:, None],
            odd_first[None] * even_b[:, None],
            even_real[None] * odd_second[:, None],
            even_imag[None] * odd_second[:, None],
        ],
        axis=1,
    )
    symbol = jnp.dot(
        factors.reshape(8 * HALF, -1), cell_factor, precision=HIGHEST_PRECISION
    ).reshape(2, 4, HALF, rows * NY)
    damp = DAMPING / (HALF * HALF) * jnp.stack(
        [slots * slots, slots_b * slots_b], axis=1
    ).reshape(4).astype(F32)
    return symbol, damp


def off_chip(value):
    return pltpu.with_memory_space_constraint(value, pltpu.HBM)


def stage_forward(density, table):
    planes, points, cells = density.shape
    sent = call(
        forward_kernel,
        [((points * planes, cells), F32)],
        (off_chip(density), off_chip(table["forward_second"])),
        (
            pltpu.VMEM(density.shape, F32),
            pltpu.VMEM((points, 2 * points), BF16),
            pltpu.SemaphoreType.DMA((FORWARD_STEPS + 1,)),
        ),
        flops=6 * points * points * planes * cells,
        keep=False,
        in_specs=[pl.BlockSpec(memory_space=pl.ANY)] * 2,
    )
    return sent.reshape(points // 4, 4, planes, cells)


def stage_local(density, table):
    planes, points, cells = density.shape
    friction, shift = table["friction"], table["column_shift"]
    return call(
        local_kernel,
        [((planes, points, cells), F32)],
        (off_chip(density), off_chip(friction), off_chip(shift)),
        flops=6 * points * points * planes * cells,
        grid=(LOCAL_STEPS,),
        in_specs=[
            pl.BlockSpec((planes // LOCAL_STEPS, points, cells), lambda i: (i, 0, 0)),
            pl.BlockSpec(friction.shape, lambda i: (0, 0)),
            pl.BlockSpec(shift.shape, lambda i: (0, 0, 0)),
        ],
    )


def stage_halo(odd, columns):
    cells = columns.shape[3]
    return call(
        halo_kernel, [((POINTS + POINTS // 4, cells), F32)] * 2, (odd, columns), smem=1
    )


def stage_middle(damp, columns, symbol, table):
    _, _, _, cells = columns.shape
    width = 8 * cells
    scratch = pltpu.VMEM((2 * POINTS, width), BF16)
    return call(
        middle_kernel,
        [(columns.shape, F32)],
        (
            damp,
            columns,
            table["forward_first"],
            symbol,
            table["inverse_first"],
            table["row_inner"],
        ),
        (scratch, scratch),
        20 * POINTS * POINTS * width,
        smem=1,
    )


def stage_edge_first(odd, partial, halo):
    members, _, planes, cells = partial.shape
    return call(
        functools.partial(edge_kernel, 0),
        [((members // 2, 4, planes, cells), F32)],
        (odd, partial, halo),
        flops=20 * partial.size,
        smem=1,
    )


def stage_edge_second(odd, partial, halo, done):
    members, _, planes, cells = partial.shape

    def place(i, odd_ref):
        return (jnp.where(odd_ref[0] == 1, i, 1 - i), 0, 0, 0)

    return pl.pallas_call(
        edge_second_kernel,
        out_shape=jax.ShapeDtypeStruct(partial.shape, F32),
        grid_spec=pltpu.PrefetchScalarGridSpec(
            num_scalar_prefetch=1,
            grid=(2,),
            in_specs=[VMEM_SPEC] * 3,
            out_specs=pl.BlockSpec((members // 2, 4, planes, cells), place),
        ),
        cost_estimate=pl.CostEstimate(
            flops=20 * partial.size, bytes_accessed=4 * partial.size, transcendentals=0
        ),
        compiler_params=pltpu.CompilerParams(vmem_limit_bytes=24 << 20),
        name="edge_second",
    )(odd, on_chip(partial), on_chip(halo), on_chip(done))


def stage_backward(panels, here, table):
    planes, points, cells = here.shape
    return call(
        backward_kernel,
        [((planes, points, cells), F32)],
        (
            on_chip(panels.reshape(points * planes, cells)),
            on_chip(here),
            on_chip(table["inverse_second"]),
        ),
        flops=6 * points * points * planes * cells,
        keep=False,
        grid=(BACKWARD_STEPS,),
        in_specs=[VMEM_SPEC] * 3,
        out_specs=[
            pl.BlockSpec((planes // BACKWARD_STEPS, points, cells), lambda i: (i, 0, 0))
        ],
    )


def local(density, mode_waves, mode_amplitudes, mode_phases):
    _, _, cells = density.shape
    rows_dev = cells // NY
    group = ("pair", "mom")
    strips = lax.axis_size("y")
    table = tables(rows_dev)

    sent = stage_forward(density, table)
    columns = lax.all_to_all(sent, group, split_axis=0, concat_axis=0, tiled=True)
    here = stage_local(density, table)
    position = lax.axis_index("pair") * lax.axis_size("mom") + lax.axis_index("mom")
    odd = (lax.axis_index("y") % 2).reshape(1)
    symbol, damp = symbol_table(
        mode_waves,
        mode_amplitudes,
        mode_phases,
        2 * position,
        lax.axis_index("y") * (2 * rows_dev),
        2 * rows_dev,
        2 * rows_dev * strips,
    )
    first, second = stage_halo(odd, columns)
    links = [(i, (i + 1) % strips) for i in range(strips)]
    swaps = [[p for l in links[start::2] for p in (l, l[::-1])] for start in range(2)]
    first = lax.ppermute(first, "y", swaps[0])
    second = lax.ppermute(second, "y", swaps[1])
    partial = stage_middle(damp, columns, symbol, table)
    done = stage_edge_first(odd, partial, first)
    back = stage_edge_second(odd, partial, second, done)
    panels = lax.all_to_all(back, group, split_axis=0, concat_axis=0, tiled=True)
    return stage_backward(panels, here, table)


def solution(mesh):
    bands = mesh.shape["space"]
    finer = jax.sharding.Mesh(
        mesh.devices.reshape(bands // 2, 2, mesh.shape["mom"]), ("y", "pair", "mom")
    )
    return jax.shard_map(
        local,
        mesh=finer,
        in_specs=(P("mom", None, ("y", "pair")), P(), P(), P()),
        out_specs=P("mom", None, ("y", "pair")),
        check_vma=False,
    )
```

```python
import functools
import math

import jax
import jax.numpy as jnp
import ml_dtypes
import numpy as np
from jax import lax
from jax.experimental import pallas as pl
from jax.experimental.pallas import tpu as pltpu
from jax.sharding import PartitionSpec as P

NY = 16
POINTS = 256
HALF = POINTS // 2
DAMPING = 0.5
FRICTION = 0.5
MINUS = ((-3, -2.0), (-2, 15.0), (-1, -60.0), (0, 20.0), (1, 30.0), (2, -3.0))
PLUS = ((3, 2.0), (2, -15.0), (1, 60.0), (0, -20.0), (-1, -30.0), (-2, 3.0))
F32 = jnp.float32
BF16 = jnp.bfloat16
HIGHEST_PRECISION = lax.Precision.HIGHEST
BACKWARD_STEPS = 1
LOCAL_STEPS = 2


def wide(table):
    high = table.astype(ml_dtypes.bfloat16)
    low = (table - high.astype(np.float64)).astype(ml_dtypes.bfloat16)
    return np.concatenate([high, low], axis=1)


def real_fourier():
    k = np.arange(POINTS)
    m = np.arange(HALF)
    angles = 2.0 * np.pi / POINTS * (m[:, None] * k[None, :] % POINTS)
    cosine, sine = np.cos(angles), -np.sin(angles)
    sine[0] = 1.0 - 2.0 * (k % 2)
    forward = np.concatenate([cosine, sine], axis=0)
    weight = np.full((HALF,), 2.0)
    weight[0] = 1.0
    inverse = (forward * np.concatenate([weight, weight])[:, None] / POINTS).T
    return forward, inverse


def interleaved(rows):
    return np.stack([rows[:HALF], rows[HALF:]], axis=1).reshape(POINTS, -1)


def friction_matrix():
    speed = (2.0 * np.arange(POINTS) - POINTS + 1) / POINTS
    result = np.zeros((POINTS, POINTS))
    k = np.arange(POINTS - 1)
    result[k, k + 1] = FRICTION * speed[k + 1]
    result[k + 1, k] = -FRICTION * speed[k]
    return result


def row_matrix(stencil, rows):
    result = np.zeros((rows * NY, rows * NY))
    for out_row in range(rows):
        for offset, weight in stencil:
            row = out_row + offset
            if 0 <= row < rows:
                for column in range(NY):
                    result[row * NY + column, out_row * NY + column] = weight
    return result


def column_matrix(stencil, rows):
    result = np.zeros((rows * NY, rows * NY))
    for row in range(rows):
        for column in range(NY):
            for offset, weight in stencil:
                result[row * NY + (column + offset) % NY, row * NY + column] += weight
    return result


def bf16_table(table):
    return jnp.asarray(table.astype(ml_dtypes.bfloat16))


def tables(rows_dev):
    forward, inverse = real_fourier()
    result = {}
    result["forward_second"] = jnp.asarray(wide(interleaved(forward)))
    result["inverse_second"] = jnp.asarray(wide(interleaved(inverse.T).T))
    result["forward_first"] = jnp.asarray(wide(forward))
    friction = friction_matrix().astype(ml_dtypes.bfloat16)
    result["inverse_first"] = jnp.asarray(wide(inverse))
    result["friction"] = jnp.asarray(np.concatenate([friction, friction], axis=1))
    rows = 2 * rows_dev
    result["row_inner"] = bf16_table(
        np.stack([row_matrix(stencil, rows) for stencil in (PLUS, MINUS)])
    )
    result["column_shift"] = bf16_table(
        np.stack(
            [
                np.concatenate([column_matrix(s, rows_dev)] * 2, axis=0)
                for s in (PLUS, MINUS)
            ]
        )
    )
    return result


def split(value):
    high = value.astype(BF16)
    low = (value - high.astype(F32)).astype(BF16)
    return high, low


def dot(left, right):
    return jnp.dot(left, right, preferred_element_type=F32)


def wide_dot(table, high, low):
    first, second = table[:, :POINTS], table[:, POINTS : 2 * POINTS]
    return dot(
        jnp.concatenate([first, first, second], axis=1),
        jnp.concatenate([high, low, high], axis=0),
    )


def speed_over_60(first, count, width):
    index = first + lax.broadcasted_iota(jnp.int32, (count, width), 0)
    return (2 * index - (POINTS - 1)).astype(F32) * (1.0 / (60 * POINTS))


def forward_kernel(u_ref, table_ref, out_ref):
    planes, _, cells = u_ref.shape
    parts = [split(u_ref[k]) for k in range(planes)]
    high, low = (jnp.concatenate(values, axis=1) for values in zip(*parts))
    result = wide_dot(table_ref[...], high, low)
    for k in range(planes):
        out_ref[pl.ds(k, POINTS, stride=planes), :] = result[:, k * cells : (k + 1) * cells]


def backward_kernel(w_ref, local_ref, table_ref, out_ref):
    planes, _, cells = out_ref.shape
    first = pl.program_id(0) * planes
    stride = w_ref.shape[0] // POINTS
    parts = [
        split(w_ref[pl.ds(first + k, POINTS, stride=stride), :]) for k in range(planes)
    ]
    high, low = (jnp.concatenate(values, axis=1) for values in zip(*parts))
    result = wide_dot(table_ref[...], high, low)
    for k in range(planes):
        out_ref[k] = result[:, k * cells : (k + 1) * cells] + local_ref[first + k]


def local_kernel(u_ref, friction_ref, shift_ref, out_ref):
    planes, _, cells = u_ref.shape
    first = pl.program_id(0) * planes
    for k in range(planes):
        high, low = split(u_ref[k])
        friction = dot(friction_ref[...], jnp.concatenate([high, low], axis=0))
        both = jnp.concatenate([high, low], axis=1)
        for side in range(2):
            part = slice(side * HALF, (side + 1) * HALF)
            moved = dot(both[part], shift_ref[side])
            out_ref[first + k, part, :] = friction[part] - moved * speed_over_60(
                side * HALF, HALF, cells
            )


def lane_select(values, lane, width):
    result = values[0]
    for index, value in enumerate(values[1:], 1):
        result = jnp.where(lane >= index * width, value, result)
    return result


def turn(value, shift):
    shift %= value.shape[1]
    return pltpu.roll(value, shift, 1) if shift else value


def pack(r_ref, near, far, side):
    cells = r_ref.shape[3]
    lane = lax.broadcasted_iota(jnp.int32, (POINTS, cells), 1)
    columns = [r_ref[:, q].reshape(POINTS, cells) for q in range(4)]
    wide_part = lane_select(
        [turn(v, 2 * NY * q - near) for q, v in enumerate(columns)], lane, 2 * NY
    )
    quarter = HALF // 2
    lane = lane[:quarter]
    thin_part = lane_select(
        [
            turn(columns[q][side * HALF + h * quarter : side * HALF + (h + 1) * quarter], NY * (q + 4 * h) - far)
            for h in range(2)
            for q in range(4)
        ],
        lane,
        NY,
    )
    return wide_part, thin_part


def halo_kernel(odd_ref, r_ref, first_ref, second_ref):
    owners = r_ref.shape[0] // 2
    cells = r_ref.shape[3]
    odd = odd_ref[0] == 1
    up = pack(r_ref.at[owners:], cells - 2 * NY, cells - 3 * NY, 1)
    down = pack(r_ref.at[:owners], 0, 2 * NY, 0)
    at = 0
    for upper, lower in zip(up, down):
        rows = upper.shape[0]
        first_ref[at : at + rows, :] = jnp.where(odd, lower, upper)
        second_ref[at : at + rows, :] = jnp.where(odd, upper, lower)
        at += rows


def load_columns(r_ref, x_ref):
    owners = r_ref.shape[0] // 2
    cells = r_ref.shape[3]
    for q in range(4):
        for side in range(2):
            value = r_ref[side * owners : (side + 1) * owners, q].reshape(POINTS, cells)
            high, low = split(value)
            at = (2 * q + side) * cells
            x_ref[0:POINTS, at : at + cells] = high
            x_ref[POINTS : 2 * POINTS, at : at + cells] = low


def first_friction(value):
    index = lax.broadcasted_iota(jnp.int32, value.shape, 0)
    weighted = value * (
        (2 * index - (POINTS - 1)).astype(F32) * (FRICTION / POINTS)
    )
    later = jnp.where(index < POINTS - 1, pltpu.roll(weighted, POINTS - 1, 0), 0.0)
    earlier = jnp.where(index > 0, pltpu.roll(weighted, 1, 0), 0.0)
    return later - earlier


def middle_kernel(
    damp_ref, r_ref, forward_ref, symbol_ref, inverse_ref, inner_ref, out_ref, x_ref, y_ref
):
    load_columns(r_ref, x_ref)
    spectrum = wide_dot(forward_ref[...], x_ref[0:POINTS, :], x_ref[POINTS:, :])
    width = spectrum.shape[1] // 4
    row = lax.broadcasted_iota(jnp.int32, (HALF, width), 0)
    scale = DAMPING / (HALF * HALF)
    damp_real = scale * (row * row).astype(F32)
    row_imag = jnp.where(row == 0, HALF, row)
    damp_imag = scale * (row_imag * row_imag).astype(F32)
    for slot in range(2):
        qa, qb = 2 * slot, 2 * slot + 1
        real_a, imag_a = (
            spectrum[h * HALF : (h + 1) * HALF, qa * width : (qa + 1) * width]
            for h in range(2)
        )
        real_b, imag_b = (
            spectrum[h * HALF : (h + 1) * HALF, qb * width : (qb + 1) * width]
            for h in range(2)
        )
        odd_a, odd_b = symbol_ref[slot, 0], symbol_ref[slot, 1]
        even_real, even_imag = symbol_ref[slot, 2], symbol_ref[slot, 3]
        da, db = damp_ref[qa], damp_ref[qb]
        results = (
            (qa, 0, -odd_a * imag_a - even_real * real_b - (damp_real + da) * real_a),
            (qa, 1, odd_a * real_a - even_imag * imag_b - (damp_imag + da) * imag_a),
            (qb, 0, -odd_b * imag_b + even_real * real_a - (damp_real + db) * real_b),
            (qb, 1, odd_b * real_b + even_imag * imag_a - (damp_imag + db) * imag_b),
        )
        for q, half, value in results:
            high, low = split(value)
            at = q * width
            y_ref[half * HALF : (half + 1) * HALF, at : at + width] = high
            y_ref[POINTS + half * HALF : POINTS + (half + 1) * HALF, at : at + width] = low
    cells = width // 2
    owners = out_ref.shape[0] // 2
    result = wide_dot(inverse_ref[...], y_ref[0:POINTS, :], y_ref[POINTS:, :])
    moved = [
        dot(
            jnp.concatenate(
                [
                    jnp.concatenate(
                        [
                            x_ref[
                                half + side * HALF : half + (side + 1) * HALF,
                                q * width : (q + 1) * width,
                            ]
                            for half in (0, POINTS)
                        ],
                        axis=1,
                    )
                    for q in range(4)
                ],
                axis=0,
            ),
            jnp.concatenate([inner_ref[side]] * 2, axis=0),
        )
        for side in range(2)
    ]
    rows = owners // 2
    for q in range(4):
        for band in range(2):
            here = r_ref[band * owners : (band + 1) * owners, q].reshape(POINTS, cells)
            friction = first_friction(here)
            inside = slice(band * cells, (band + 1) * cells)
            for side in range(2):
                part = slice(side * HALF, (side + 1) * HALF)
                value = (
                    result[part, q * width : (q + 1) * width][:, inside]
                    + friction[part]
                    - moved[side][q * HALF : (q + 1) * HALF, inside]
                    * speed_over_60(side * HALF, HALF, cells)
                )
                at = band * owners + side * rows
                out_ref[at : at + rows, q] = value.reshape(rows, -1, cells)


def lane_weight(lane, first_row, last_row, weight):
    return jnp.where((lane >= first_row * NY) & (lane < last_row * NY), weight, 0.0)


def edge_kernel(odd_band, odd_ref, partial_ref, halo_ref, *refs):
    out_ref = refs[-1]
    for odd in range(2):

        @pl.when(odd_ref[0] == odd)
        def _(band=odd_band if odd else 1 - odd_band):
            for side in range(2):
                edge_part(band, side, partial_ref, halo_ref, out_ref)


def edge_part(band, side, partial_ref, halo_ref, out_ref):
    members, _, _, cells = out_ref.shape
    owners = members // 2
    band_rows = cells // NY
    stencil = dict((PLUS, MINUS)[side])
    weights = [stencil.get(s if band else -s) for s in (1, 2, 3)]
    lane = lax.broadcasted_iota(jnp.int32, (HALF, cells), 1)
    pair = halo_ref[side * HALF : (side + 1) * HALF, :]
    thin = halo_ref[POINTS : POINTS + HALF // 2, :]
    speed = speed_over_60(side * HALF, HALF, cells)
    here = slice(side * owners, (side + 1) * owners)
    block = slice((2 * band + side) * owners, (2 * band + side + 1) * owners)
    for q in range(4):
        moved = 0.0
        for s, weight in enumerate(weights, 1):
            if weight is None:
                continue
            if band:
                near = band_rows - s
                rows = (near, min(near + 2, band_rows))
            else:
                near = s - 2
                rows = (max(near, 0), s)
            moved += lane_weight(lane, *rows, weight) * turn(pair, NY * (near - 2 * q))
        if weights[2] is not None:
            row = band_rows - 1 if band else 0
            third = jnp.concatenate(
                [turn(thin, NY * (row - q - 4 * h)) for h in range(2)], axis=0
            )
            moved += lane_weight(lane, row, row + 1, weights[2]) * third
        out_ref[here, q] = partial_ref[block, q] - (moved * speed).reshape(owners, -1, cells)


VMEM_SPEC = pl.BlockSpec(memory_space=pltpu.VMEM)
SMEM_SPEC = pl.BlockSpec(memory_space=pltpu.SMEM)


def on_chip(value):
    return pltpu.with_memory_space_constraint(value, pltpu.VMEM)


def call(
    kernel,
    shapes,
    inputs,
    scratch=(),
    flops=1,
    smem=0,
    keep=True,
    grid=(),
    in_specs=None,
    out_specs=None,
):
    bytes_accessed = sum(v.size * v.dtype.itemsize for v in inputs)
    shapes = [pltpu.VMEM(*s) if keep else jax.ShapeDtypeStruct(*s) for s in shapes]
    if in_specs is None:
        inputs = [*inputs[:smem], *(on_chip(v) for v in inputs[smem:])]
        in_specs = [SMEM_SPEC] * smem + [VMEM_SPEC] * (len(inputs) - smem)
    if out_specs is None:
        out_specs = [VMEM_SPEC] * len(shapes)
    single = len(shapes) == 1
    return pl.pallas_call(
        kernel,
        grid=grid,
        out_shape=shapes[0] if single else shapes,
        in_specs=in_specs,
        out_specs=out_specs[0] if single else out_specs,
        scratch_shapes=list(scratch),
        cost_estimate=pl.CostEstimate(
            flops=flops, bytes_accessed=2 * bytes_accessed, transcendentals=0
        ),
        compiler_params=pltpu.CompilerParams(vmem_limit_bytes=24 << 20),
    )(*inputs)


def symbol_table(mode_waves, mode_amplitudes, mode_phases, first_slot, first_row, rows, total_rows):
    local = jnp.arange(rows * NY, dtype=jnp.int32)
    row, column = first_row + local // NY, local % NY
    turn_rows = mode_waves[:, 0:1] * row[None, :] % total_rows
    turn_columns = mode_waves[:, 1:2] * column[None, :] % NY
    angles = (
        2.0
        * math.pi
        * (turn_rows.astype(F32) / total_rows + turn_columns.astype(F32) / NY)
        + mode_phases[:, None]
    )
    cell_factor = mode_amplitudes[:, None] * jnp.sin(angles)
    scale = math.pi / POINTS

    def turned(waves, frequency):
        return scale * (waves * frequency % (2 * POINTS)).astype(F32)

    first_waves, second_waves = mode_waves[None, :, 0], mode_waves[None, :, 1]
    real_freq = jnp.arange(HALF, dtype=jnp.int32)[:, None]
    imag_freq = jnp.where(real_freq == 0, HALF, real_freq)
    odd_first = jnp.sin(turned(first_waves, real_freq))
    even_real = jnp.cos(turned(first_waves, real_freq))
    even_imag = jnp.cos(turned(first_waves, imag_freq))
    slots = first_slot + jnp.arange(2, dtype=jnp.int32)[:, None]
    slots_b = jnp.where(slots == 0, HALF, slots)
    odd_second = jnp.sin(turned(second_waves, slots))
    even_a = jnp.cos(turned(second_waves, slots))
    even_b = jnp.cos(turned(second_waves, slots_b))
    factors = jnp.stack(
        [
            odd_first[None] * even_a[:, None],
            odd_first[None] * even_b[:, None],
            even_real[None] * odd_second[:, None],
            even_imag[None] * odd_second[:, None],
        ],
        axis=1,
    )
    symbol = jnp.dot(
        factors.reshape(8 * HALF, -1), cell_factor, precision=HIGHEST_PRECISION
    ).reshape(2, 4, HALF, rows * NY)
    damp = DAMPING / (HALF * HALF) * jnp.stack(
        [slots * slots, slots_b * slots_b], axis=1
    ).reshape(4).astype(F32)
    return symbol, damp


def off_chip(value):
    return pltpu.with_memory_space_constraint(value, pltpu.HBM)


def stage_forward(density, table):
    planes, points, cells = density.shape
    sent = call(
        forward_kernel,
        [((points * planes, cells), F32)],
        (off_chip(density), off_chip(table["forward_second"])),
        flops=6 * points * points * planes * cells,
        keep=False,
        in_specs=[VMEM_SPEC] * 2,
    )
    return sent.reshape(points // 4, 4, planes, cells)


def stage_local(density, table):
    planes, points, cells = density.shape
    friction, shift = table["friction"], table["column_shift"]
    return call(
        local_kernel,
        [((planes, points, cells), F32)],
        (off_chip(density), off_chip(friction), off_chip(shift)),
        flops=6 * points * points * planes * cells,
        grid=(LOCAL_STEPS,),
        in_specs=[
            pl.BlockSpec((planes // LOCAL_STEPS, points, cells), lambda i: (i, 0, 0)),
            pl.BlockSpec(friction.shape, lambda i: (0, 0)),
            pl.BlockSpec(shift.shape, lambda i: (0, 0, 0)),
        ],
    )


def stage_halo(odd, columns):
    cells = columns.shape[3]
    return call(
        halo_kernel, [((POINTS + POINTS // 4, cells), F32)] * 2, (odd, columns), smem=1
    )


def stage_middle(damp, columns, symbol, table):
    _, _, _, cells = columns.shape
    width = 8 * cells
    scratch = pltpu.VMEM((2 * POINTS, width), BF16)
    return call(
        middle_kernel,
        [(columns.shape, F32)],
        (
            damp,
            columns,
            table["forward_first"],
            symbol,
            table["inverse_first"],
            table["row_inner"],
        ),
        (scratch, scratch),
        20 * POINTS * POINTS * width,
        smem=1,
    )


def stage_edge(odd, partial, halo, odd_band, back=None):
    members, _, planes, cells = partial.shape

    def place(_, odd_ref):
        return (jnp.where(odd_ref[0] == 1, odd_band, 1 - odd_band), 0, 0, 0)

    given = [] if back is None else [off_chip(back)]
    return pl.pallas_call(
        functools.partial(edge_kernel, odd_band),
        out_shape=pltpu.HBM(partial.shape, F32),
        grid_spec=pltpu.PrefetchScalarGridSpec(
            num_scalar_prefetch=1,
            grid=(1,),
            in_specs=[VMEM_SPEC] * 2 + [pl.BlockSpec(memory_space=pl.ANY)] * len(given),
            out_specs=pl.BlockSpec((members // 2, 4, planes, cells), place),
        ),
        input_output_aliases={3: 0} if given else {},
        cost_estimate=pl.CostEstimate(
            flops=20 * partial.size, bytes_accessed=4 * partial.size, transcendentals=0
        ),
        compiler_params=pltpu.CompilerParams(vmem_limit_bytes=24 << 20),
        name="edge_second" if given else "edge_first",
    )(odd, on_chip(partial), on_chip(halo), *given)


def stage_backward(panels, here, table):
    planes, points, cells = here.shape
    return call(
        backward_kernel,
        [((planes, points, cells), F32)],
        (
            on_chip(panels.reshape(points * planes, cells)),
            on_chip(here),
            on_chip(table["inverse_second"]),
        ),
        flops=6 * points * points * planes * cells,
        keep=False,
        grid=(BACKWARD_STEPS,),
        in_specs=[VMEM_SPEC] * 3,
        out_specs=[
            pl.BlockSpec((planes // BACKWARD_STEPS, points, cells), lambda i: (i, 0, 0))
        ],
    )


def local(density, mode_waves, mode_amplitudes, mode_phases):
    _, _, cells = density.shape
    rows_dev = cells // NY
    group = ("pair", "mom")
    strips = lax.axis_size("y")
    table = tables(rows_dev)

    sent = stage_forward(density, table)
    columns = lax.all_to_all(sent, group, split_axis=0, concat_axis=0, tiled=True)
    here = stage_local(density, table)
    position = lax.axis_index("pair") * lax.axis_size("mom") + lax.axis_index("mom")
    odd = (lax.axis_index("y") % 2).reshape(1)
    symbol, damp = symbol_table(
        mode_waves,
        mode_amplitudes,
        mode_phases,
        2 * position,
        lax.axis_index("y") * (2 * rows_dev),
        2 * rows_dev,
        2 * rows_dev * strips,
    )
    first, second = stage_halo(odd, columns)
    links = [(i, (i + 1) % strips) for i in range(strips)]
    swaps = [[p for l in links[start::2] for p in (l, l[::-1])] for start in range(2)]
    first = lax.ppermute(first, "y", swaps[0])
    second = lax.ppermute(second, "y", swaps[1])
    partial = stage_middle(damp, columns, symbol, table)
    back = stage_edge(odd, partial, first, 0)
    back = stage_edge(odd, partial, second, 1, back)
    panels = lax.all_to_all(back, group, split_axis=0, concat_axis=0, tiled=True)
    return stage_backward(panels, here, table)


def solution(mesh):
    bands = mesh.shape["space"]
    finer = jax.sharding.Mesh(
        mesh.devices.reshape(bands // 2, 2, mesh.shape["mom"]), ("y", "pair", "mom")
    )
    return jax.shard_map(
        local,
        mesh=finer,
        in_specs=(P("mom", None, ("y", "pair")), P(), P(), P()),
        out_specs=P("mom", None, ("y", "pair")),
        check_vma=False,
    )
```
